32 devices in a mesh: dp: 16 (over z, y, core), tensor: 2 (over x).
Axes of the slice: x: 2, y: 2, z: 4, core: 2. Of those that a mesh axis runs over, the one named last changes fastest.
Arguments:
- queries: bfloat16 [16, 64, 64, 128], P('dp', None, 'tensor'), may hold values from -6 to 6
- tree_keys: bfloat16 [16, 64, 8, 128], P('dp', None, 'tensor'), may hold values from -6 to 6
- tree_values: bfloat16 [16, 64, 8, 128], P('dp', None, 'tensor'), may hold values from -6 to 6
- cache_keys: bfloat16 [16, 8192, 8, 128], P('dp', None, 'tensor'), may hold values from -6 to 6
- cache_values: bfloat16 [16, 8192, 8, 128], P('dp', None, 'tensor'), may hold values from -6 to 6
- cache_len: int32 [16], P('dp'), may hold values from 1024 to 8192, as said below
- tree_parent: int32 [16, 64], P('dp'), may hold values from -1 to 62, as said below
- path_nodes: int32 [16, 8], P('dp'), may hold values from 0 to 63, as said below
- path_len: int32 [16], P('dp'), may hold values from 1 to 8, as said below
- out_weight: bfloat16 [8192, 8192], P('tensor', 'dp'), may hold values from -1 to 1
- norm_gain: float32 [8192], P('dp'), may hold values from 0.5 to 1.5
Outputs:
- verify_out: bfloat16 [16, 64, 8192], P('dp', None, 'tensor')
- paths_hidden: bfloat16 [128, 8192], P('tensor', 'dp')
The draws below stay inside these ranges and needn't reach their ends.
Inputs may be any that keep to these rules, and one draw needn't show every extreme that they name: `cache_len`: some row has exactly 8192. tree_parent[r, 0] = -1 marks the root; every other token's parent has a lower index. path_nodes[r, 0] = 0, and for 0 < k < path_len[r] path_nodes[r, k] is a child of path_nodes[r, k - 1]; slots k >= path_len[r] hold 0. `path_len`: some row has the full 8.
All inputs are finite; a program needn't handle non-finite values.
Results may differ from the reference program's by a relative error of at most 0.015.
Values may be sent and summed in bfloat16 or wider, within the bound.
No kernel may reach another device: no remote copies, remote signals or barrier semaphores. Data moves between devices by JAX's collectives and lax.ppermute only.
A program may use at most 192 MiB of HBM per device.

```python
import math
import jax
import jax.numpy as jnp
from jax import lax

D = 8192
H = 64
KVH = 8
HD = 128
TREE = 64
DEPTH = 8
CACHE = 8192
ROWS = 16


def shared_direction(key):
    return 0.6 * jax.random.normal(jax.random.fold_in(key, 7), (ROWS, 1, KVH, HD), jnp.float32)


def draw_queries(key, part):
    noise_key = jax.random.fold_in(key, 3)
    base_draw = jax.random.normal(noise_key, (ROWS, TREE, H, HD), jnp.float32)
    common = jnp.repeat(shared_direction(key), H // KVH, axis=2)
    result = jnp.clip(base_draw + common, -6.0, 6.0)
    return result.astype(jnp.bfloat16)


def draw_tree_keys(key, part):
    noise_key = jax.random.fold_in(key, 4)
    base_draw = jax.random.normal(noise_key, (ROWS, TREE, KVH, HD), jnp.float32)
    return jnp.clip(base_draw + shared_direction(key), -6.0, 6.0).astype(jnp.bfloat16)


def draw_cache_keys(key, part):
    noise_key = jax.random.fold_in(key, 5)
    result = jnp.clip(jax.random.normal(noise_key, (ROWS, CACHE, KVH, HD), jnp.float32), -6.0, 6.0)
    return result.astype(jnp.bfloat16)


def draw_cache_len(key, part):
    lowest = max(CACHE // 8, 2)
    lengths = jax.random.randint(jax.random.fold_in(key, 21), (ROWS,), lowest, CACHE + 1, jnp.int32)
    return lengths.at[0].set(CACHE)


def tree_draws(key):
    width = max(1, TREE // (2 * DEPTH))
    node_ids = jnp.arange(TREE, dtype=jnp.int32)
    lowest = jnp.maximum(node_ids - width, 0)
    spans = jnp.maximum(node_ids - lowest, 1)
    raw_bits = jax.random.randint(jax.random.fold_in(key, 11), (ROWS, TREE), 0, 1 << 20, jnp.int32)
    parents = lowest[None, :] + raw_bits % spans[None, :]
    parents = parents.at[:, 0].set(-1)
    depths = jnp.zeros((ROWS, TREE), jnp.int32)
    for node in range(1, TREE):
        above = parents[:, node]
        depths = depths.at[:, node].set(jnp.take_along_axis(depths, above[:, None], axis=1)[:, 0] + 1)
    lengths = jax.random.randint(jax.random.fold_in(key, 12), (ROWS,), 1, DEPTH + 1, jnp.int32)
    lengths = lengths.at[0].set(DEPTH)
    ends = jax.random.randint(jax.random.fold_in(key, 13), (ROWS,), TREE // 2, TREE, jnp.int32)
    chain = [ends]
    current = ends
    for climb in range(TREE - 1):
        upper = jnp.take_along_axis(parents, jnp.maximum(current, 0)[:, None], axis=1)[:, 0]
        current = jnp.where(current > 0, upper, 0)
        chain.append(current)
    chain = jnp.stack(chain, axis=1)
    end_depth = jnp.take_along_axis(depths, ends[:, None], axis=1)[:, 0]
    slot_ids = jnp.arange(DEPTH, dtype=jnp.int32)
    index_up = jnp.maximum(end_depth[:, None] - slot_ids[None, :], 0)
    on_path = jnp.take_along_axis(chain, index_up, axis=1)
    paths = jnp.where(slot_ids[None, :] < lengths[:, None], on_path, 0)
    parents = parents.at[0, TREE - 1].set(paths[0, DEPTH - 2])
    paths = paths.at[0, DEPTH - 1].set(TREE - 1)
    return (parents, paths, lengths)


def draw_tree_parent(key, part):
    return tree_draws(key)[0]


def draw_path_nodes(key, part):
    return tree_draws(key)[1]


def draw_path_len(key, part):
    return tree_draws(key)[2]


def draw_out_weight(key, part):
    column = jnp.arange(D, dtype=jnp.float32) / D
    noise_key = jax.random.fold_in(key, 31)
    base_draw = jnp.clip(jax.random.normal(noise_key, (H * HD, D), jnp.float32), -6.0, 6.0)
    factor = 3.0 ** (0.5 * column)
    return jnp.clip(base_draw * factor[None, :] / math.sqrt(H * HD), -1.0, 1.0).astype(jnp.bfloat16)


def block_levels(stream_key, extent, cuts, least, high):
    def one(axis_at, blocks):
        draws = jax.random.uniform(jax.random.fold_in(jax.random.fold_in(stream_key, 6), axis_at), (blocks,), jnp.float32, least / len(cuts), high / len(cuts))
        return jnp.repeat(jnp.exp(draws), extent[axis_at] // blocks).reshape((-1,) + (1,) * (len(extent) - axis_at - 1))

    loudness = one(*cuts[0])
    for cut in cuts[1:]:
        loudness = loudness * one(*cut)
    return loudness


def gaussian(rng, extent, spread, reach, split=(), kind=jnp.bfloat16):
    array = spread * jax.random.normal(rng, extent, jnp.float32)
    if split:
        array = array * block_levels(rng, extent, split, -0.22, 0.18)
    return jnp.clip(array, -reach, reach).astype(kind)


def setup_inputs(seed: int = 0) -> dict:
    key_of = jax.random.split(jax.random.key(seed), 12)
    return {
        "queries": draw_queries(jax.random.fold_in(key_of[11], 71), 0),
        "tree_keys": draw_tree_keys(jax.random.fold_in(key_of[11], 71), 0),
        "tree_values": gaussian(key_of[2], (ROWS, TREE, KVH, HD), 1.0, 6.0, ((0, 16), (2, 2))),
        "cache_keys": draw_cache_keys(jax.random.fold_in(key_of[11], 71), 0),
        "cache_values": gaussian(key_of[4], (ROWS, CACHE, KVH, HD), 1.0, 6.0, ((0, 16), (2, 2))),
        "cache_len": draw_cache_len(jax.random.fold_in(key_of[11], 71), 0),
        "tree_parent": draw_tree_parent(jax.random.fold_in(key_of[11], 71), 0),
        "path_nodes": draw_path_nodes(jax.random.fold_in(key_of[11], 71), 0),
        "path_len": draw_path_len(jax.random.fold_in(key_of[11], 71), 0),
        "out_weight": draw_out_weight(jax.random.fold_in(key_of[11], 71), 0),
        "norm_gain": jnp.clip(1.0 + 0.1 * jax.random.normal(key_of[10], (D,), jnp.float32), 0.5, 1.5),
    }


NEG_FILL = -1e+30
EPSILON = 1e-05

def ancestor_table(tree_parent):
    tree_size = tree_parent.shape[-1]
    node_ids = jnp.arange(tree_size, dtype=jnp.int32)
    parent_hot = (tree_parent[:, :, None] == node_ids[None, None, :]).astype(jnp.float32)
    reachable = parent_hot + jnp.eye(tree_size, dtype=jnp.float32)[None]
    for squaring in range(max(1, (tree_size - 1).bit_length())):
        reachable = jnp.minimum(jnp.einsum('rij,rjk->rik', reachable, reachable, precision=lax.Precision.HIGHEST), 1.0)
    return reachable > 0.5

def attend_row(operands):
    query_row, tree_key, tree_value, cache_key, cache_value, valid_len, allowed = operands
    tree_len, head_count, head_dim = query_row.shape
    cache_size, kv_heads = (cache_key.shape[0], cache_key.shape[1])
    groups = head_count // kv_heads
    grouped = query_row.astype(jnp.float32).reshape(tree_len, kv_heads, groups, head_dim)
    key_all = jnp.concatenate([cache_key, tree_key], axis=0).astype(jnp.float32)
    value_all = jnp.concatenate([cache_value, tree_value], axis=0).astype(jnp.float32)
    scores = jnp.einsum('tkgd,ckd->tkgc', grouped, key_all) * (1.0 / math.sqrt(head_dim))
    cache_ok = jnp.arange(cache_size, dtype=jnp.int32) < valid_len
    permitted = jnp.concatenate([jnp.broadcast_to(cache_ok[None, :], (tree_len, cache_size)), allowed], axis=1)
    permitted = permitted[:, None, None, :]
    scores = jnp.where(permitted, scores, NEG_FILL)
    row_max = lax.optimization_barrier(jnp.max(scores, axis=-1, keepdims=True))
    weights = jnp.where(permitted, jnp.exp(scores - row_max), 0.0)
    weight_sum = lax.optimization_barrier(jnp.sum(weights, axis=-1))
    rounded = lax.optimization_barrier(weights.astype(jnp.bfloat16)).astype(jnp.float32)
    attended = jnp.einsum('tkgc,ckd->tkgd', rounded, value_all) / weight_sum[..., None]
    return attended.reshape(tree_len, head_count * head_dim).astype(jnp.bfloat16)

def reference(queries, tree_keys, tree_values, cache_keys, cache_values, cache_len, tree_parent, path_nodes, path_len, out_weight, norm_gain):
    allowed = ancestor_table(tree_parent)
    verify_out = lax.map(attend_row, (queries, tree_keys, tree_values, cache_keys, cache_values, cache_len, allowed))
    picked = jnp.take_along_axis(verify_out, path_nodes[:, :, None], axis=1)
    slot_ids = jnp.arange(path_nodes.shape[1], dtype=jnp.int32)
    slot_live = slot_ids[None, :] < path_len[:, None]
    picked = jnp.where(slot_live[:, :, None], picked, jnp.zeros((), jnp.bfloat16))
    path_rows = picked.reshape(-1, picked.shape[-1])
    projected = jnp.dot(path_rows, out_weight, preferred_element_type=jnp.float32)
    inverse = lax.rsqrt(lax.optimization_barrier(jnp.mean(projected * projected, axis=1, keepdims=True)) + EPSILON)
    paths_hidden = (projected * inverse * norm_gain[None, :]).astype(jnp.bfloat16)
    return (verify_out, paths_hidden)
```

```python
import functools
import math

import jax
import jax.numpy as jnp
from jax import lax
from jax.experimental import pallas as pl
from jax.experimental.pallas import tpu as pltpu
from jax.sharding import PartitionSpec as P

EPSILON = 1e-05
NEG = -1e30
LIMIT = 2.0**100
F32 = jnp.float32
BF16 = jnp.bfloat16


def dot_nt(a, b):
    return lax.dot_general(a, b, (((1,), (1,)), ((), ())), preferred_element_type=F32)


def ancestors(parent_row):
    t = parent_row.shape[1]
    row = lax.broadcasted_iota(jnp.int32, (t, t), 0)
    col = lax.broadcasted_iota(jnp.int32, (t, t), 1)
    reach = jnp.where((parent_row == row) | (row == col), 1.0, 0.0)
    for _ in range(max(1, (t - 1).bit_length())):
        half = reach.astype(BF16)
        reach = jnp.minimum(jnp.dot(half, half, preferred_element_type=F32), 1.0)
    return reach.T > 0.5


def attention_kernel(
    lens,
    nodes,
    plen,
    parent_ref,
    q_ref,
    tk_ref,
    tv_ref,
    k_ref,
    v_ref,
    k_hbm,
    v_hbm,
    out_ref,
    path_ref,
    kf,
    vf,
    tf,
    p_ref,
    acc_ref,
    sh_ref,
    of,
    pf,
    kb,
    vb,
    sem,
    *,
    kvh,
    groups,
    tree,
    sub,
    slow,
    scale,
):
    n = pl.program_id(0)
    c = k_ref.shape[0] // kvh
    m = groups * tree
    hd = q_ref.shape[2]
    length = lens[0]

    def head_rows(ref, g, start, count):
        return ref[pl.ds(g + kvh * start, count, stride=kvh), :]

    def tree_values(g):
        value = tf[1, pl.ds(g, tree, stride=kvh), :].astype(BF16)
        return jnp.concatenate([value, jnp.ones((tree, hd), BF16)], axis=1)

    def tree_scores(g):
        keys = tf[0, pl.ds(g, tree, stride=kvh), :].astype(BF16)
        return dot_nt(q_ref[g], keys) * scale

    @pl.when(n == 0)
    def _():
        tf[0] = tk_ref[...].astype(F32)
        tf[1] = tv_ref[...].astype(F32)
        allowed = jnp.tile(ancestors(parent_ref[...]), (groups, 1))
        diag_row = lax.broadcasted_iota(jnp.int32, (m, tree), 0) % tree
        diag = diag_row == lax.broadcasted_iota(jnp.int32, (m, tree), 1)
        for g in range(kvh):
            s = tree_scores(g)
            shift = jnp.sum(jnp.where(diag, s, 0.0), axis=1, keepdims=True)
            sh_ref[g] = jnp.broadcast_to(shift, (m, 128))
            p = jnp.where(allowed, jnp.exp2(s - shift), 0.0).astype(BF16)
            acc_ref[g] = jnp.dot(p, tree_values(g), preferred_element_type=F32)

    @pl.when(n * c < length)
    def _():
        live = lax.broadcasted_iota(jnp.int32, (c, 128), 0) < length - n * c
        ones = jnp.where(live, 1.0, 0.0).astype(BF16)
        for i in range(c // sub):
            rows = slice(i * sub * kvh, (i + 1) * sub * kvh)
            kf[rows] = k_ref[rows].astype(F32)
        for i in range(c // sub):
            rows = slice(i * sub * kvh, (i + 1) * sub * kvh)
            vf[rows] = v_ref[rows].astype(F32)
        for g in range(kvh):
            q = q_ref[g]
            shift = sh_ref[g]
            for i in range(c // sub):
                s = dot_nt(q, head_rows(kf, g, i * sub, sub).astype(BF16))
                p = [jnp.exp2(s[:, a : a + 128] * scale - shift) for a in range(0, sub, 128)]
                p_ref[:, i * sub : (i + 1) * sub] = jnp.concatenate(p, axis=1).astype(BF16)
            value = jnp.where(live, head_rows(vf, g, 0, c), 0.0).astype(BF16)
            value = jnp.concatenate([value, ones], axis=1)
            acc_ref[g] += jnp.dot(p_ref[...], value, preferred_element_type=F32)

    @pl.when(n == pl.num_programs(0) - 1)
    def _():
        fits = jnp.max(jnp.where(acc_ref[:, :, hd:] < LIMIT, 0.0, 1.0)) < 0.5

        @pl.when(jnp.logical_not(fits))
        def _():
            allowed = jnp.tile(ancestors(parent_ref[...]), (groups, 1))
            for g in range(kvh):
                s = jnp.where(allowed, tree_scores(g), NEG)
                top = jnp.max(s, axis=1, keepdims=True)
                p = jnp.where(allowed, jnp.exp2(s - top), 0.0).astype(BF16)
                sh_ref[g] = jnp.broadcast_to(top, (m, 128))
                acc_ref[g] = jnp.dot(p, tree_values(g), preferred_element_type=F32)

            def step(i, carry):
                span = pl.ds(pl.multiple_of(i * slow * kvh, slow * kvh), slow * kvh)
                copies = (
                    pltpu.make_async_copy(k_hbm.at[span], kb, sem.at[0]),
                    pltpu.make_async_copy(v_hbm.at[span], vb, sem.at[1]),
                )
                for copy in copies:
                    copy.start()
                for copy in copies:
                    copy.wait()
                kf[: slow * kvh] = kb[...].astype(F32)
                vf[: slow * kvh] = vb[...].astype(F32)
                left = length - i * slow
                col = lax.broadcasted_iota(jnp.int32, (m, slow), 1) < left
                live = lax.broadcasted_iota(jnp.int32, (slow, 128), 0) < left
                ones = jnp.where(live, 1.0, 0.0).astype(BF16)
                for g in range(kvh):
                    s = dot_nt(q_ref[g], head_rows(kf, g, 0, slow).astype(BF16)) * scale
                    s = jnp.where(col, s, NEG)
                    old = sh_ref[g]
                    top = jnp.maximum(old, jnp.max(s, axis=1, keepdims=True))
                    shrink = jnp.exp2(old - top)
                    p = [jnp.exp2(s[:, a : a + 128] - top) for a in range(0, slow, 128)]
                    p = jnp.concatenate(p, axis=1).astype(BF16)
                    value = jnp.where(live, head_rows(vf, g, 0, slow), 0.0).astype(BF16)
                    value = jnp.concatenate([value, ones], axis=1)
                    acc_ref[g] = acc_ref[g] * jnp.concatenate([shrink, shrink], axis=1) + jnp.dot(
                        p, value, preferred_element_type=F32
                    )
                    sh_ref[g] = top
                return carry

            lax.fori_loop(0, pl.cdiv(length, slow), step, 0)

        for g in range(kvh):
            rows = acc_ref[g, :, :hd] / acc_ref[g, :, hd:]
            for h in range(groups):
                lanes = slice((g * groups + h) * hd, (g * groups + h + 1) * hd)
                part = rows[h * tree : (h + 1) * tree]
                out_ref[:, lanes] = part.astype(BF16)
                of[:, lanes] = part
        for k in range(path_ref.shape[0]):
            row = of[pl.ds(nodes[k], 1), :]
            pf[k : k + 1, :] = jnp.where(k < plen[0], row, 0.0)
        path_ref[...] = pf[...].astype(BF16)


def attention(queries, tree_keys, tree_values, cache_keys, cache_values, lens, parent, nodes, plen):
    tree, heads, hd = queries.shape[1:]
    size, kvh = cache_keys.shape[1:3]
    groups = heads // kvh
    depth = nodes.shape[1]
    m = groups * tree
    c = min(1024, size)
    sub = min(256, c)
    slow = sub
    q = queries[0].transpose(1, 0, 2).reshape(kvh, m, hd)
    flat = lambda x: x.reshape(-1, hd)
    kernel = functools.partial(
        attention_kernel,
        kvh=kvh,
        groups=groups,
        tree=tree,
        sub=sub,
        slow=slow,
        scale=math.log2(math.e) / math.sqrt(hd),
    )
    whole = lambda *shape: pl.BlockSpec(shape, lambda n, *_: (0,) * len(shape))

    def chunk(n, lens, *_):
        return (jnp.minimum(n, (lens[0] - 1) // c), 0)

    anywhere = pl.BlockSpec(memory_space=pl.ANY)
    return pl.pallas_call(
        kernel,
        grid_spec=pltpu.PrefetchScalarGridSpec(
            num_scalar_prefetch=3,
            grid=(size // c,),
            in_specs=[
                whole(1, tree),
                whole(kvh, m, hd),
                whole(tree * kvh, hd),
                whole(tree * kvh, hd),
                pl.BlockSpec((c * kvh, hd), chunk),
                pl.BlockSpec((c * kvh, hd), chunk),
                anywhere,
                anywhere,
            ],
            out_specs=[whole(tree, heads * hd), whole(depth, heads * hd)],
            scratch_shapes=[
                pltpu.VMEM((c * kvh, hd), F32),
                pltpu.VMEM((c * kvh, hd), F32),
                pltpu.VMEM((2, tree * kvh, hd), F32),
                pltpu.VMEM((m, c), BF16),
                pltpu.VMEM((kvh, m, 2 * hd), F32),
                pltpu.VMEM((kvh, m, 128), F32),
                pltpu.VMEM((tree, heads * hd), F32),
                pltpu.VMEM((depth, heads * hd), F32),
                pltpu.VMEM((slow * kvh, hd), BF16),
                pltpu.VMEM((slow * kvh, hd), BF16),
                pltpu.SemaphoreType.DMA((2,)),
            ],
        ),
        out_shape=[
            jax.ShapeDtypeStruct((tree, heads * hd), BF16),
            jax.ShapeDtypeStruct((depth, heads * hd), BF16),
        ],
        name="attention",
    )(
        lens,
        nodes.reshape(-1),
        plen,
        parent,
        q,
        flat(tree_keys),
        flat(tree_values),
        flat(cache_keys),
        flat(cache_values),
        flat(cache_keys),
        flat(cache_values),
    )


def swap(x, axis, bit):
    size = lax.axis_size(axis)
    return lax.ppermute(x, axis, [(i, i ^ bit) for i in range(size)])


def bits_down(size):
    return [1 << b for b in reversed(range((size - 1).bit_length()))]


def gather_xor(x, axis):
    order = [0]
    for bit in bits_down(lax.axis_size(axis)):
        x = jnp.concatenate([x, swap(x, axis, bit)], axis=0)
        order = order + [b ^ bit for b in order]
    return x, order


def shards(
    queries,
    tree_keys,
    tree_values,
    cache_keys,
    cache_values,
    cache_len,
    tree_parent,
    path_nodes,
    path_len,
    out_weight,
    norm_gain,
):
    verify, picked = attention(
        queries, tree_keys, tree_values, cache_keys, cache_values, cache_len, tree_parent, path_nodes, path_len
    )
    dp = lax.axis_size("dp")
    tensor = lax.axis_size("tensor")
    depth = path_nodes.shape[1]
    width = dp * out_weight.shape[1]
    rows, order = gather_xor(picked, "dp")
    projected = jnp.dot(rows, out_weight, preferred_element_type=F32)
    position = [0] * dp
    for at, block in enumerate(order):
        position[block] = at
    blocks = jnp.arange(dp, dtype=jnp.int32) ^ lax.axis_index("dp")
    projected = projected.reshape(dp, depth, -1)[jnp.asarray(position, jnp.int32)[blocks]]
    projected = projected.reshape(dp * depth, -1)
    tokens = dp * depth // tensor
    if tensor == 2:
        mine = lax.axis_index("tensor")
        away = lax.dynamic_slice_in_dim(projected, (1 - mine) * tokens, tokens, 0)
        kept = lax.dynamic_slice_in_dim(projected, mine * tokens, tokens, 0)
        summed = kept + swap(away.astype(BF16), "tensor", 1).astype(F32)
    else:
        summed = lax.psum_scatter(projected.astype(BF16), "tensor", tiled=True).astype(F32)
    squares = jnp.sum(summed * summed, axis=1)
    for bit in bits_down(dp):
        squares = squares + swap(squares, "dp", bit)
    inverse = lax.rsqrt(squares / width + EPSILON)
    hidden = summed * inverse[:, None] * norm_gain[None, :]
    return (verify[None], hidden.astype(BF16))


def solution(mesh):
    return jax.shard_map(
        shards,
        mesh=mesh,
        in_specs=(
            P("dp", None, "tensor", None),
            P("dp", None, "tensor", None),
            P("dp", None, "tensor", None),
            P("dp", None, "tensor", None),
            P("dp", None, "tensor", None),
            P("dp"),
            P("dp", None),
            P("dp", None),
            P("dp"),
            P("tensor", "dp"),
            P("dp"),
        ),
        out_specs=(P("dp", None, "tensor"), P("tensor", "dp")),
        check_vma=False,
    )
```

```python
import functools
import math

import jax
import jax.numpy as jnp
from jax import lax
from jax.experimental import pallas as pl
from jax.experimental.pallas import tpu as pltpu
from jax.sharding import PartitionSpec as P

EPSILON = 1e-05
NEG = -1e30
LIMIT = 2.0**100
F32 = jnp.float32
BF16 = jnp.bfloat16


def dot_nt(a, b):
    return lax.dot_general(a, b, (((1,), (1,)), ((), ())), preferred_element_type=F32)


def ancestors(parent_row):
    t = parent_row.shape[1]
    row = lax.broadcasted_iota(jnp.int32, (t, t), 0)
    col = lax.broadcasted_iota(jnp.int32, (t, t), 1)
    reach = jnp.where((parent_row == row) | (row == col), 1.0, 0.0)
    for _ in range(max(1, (t - 1).bit_length())):
        half = reach.astype(BF16)
        reach = jnp.minimum(jnp.dot(half, half, preferred_element_type=F32), 1.0)
    return reach.T > 0.5


def attention_kernel(
    lens,
    nodes,
    plen,
    parent_ref,
    tk_ref,
    tv_ref,
    q_hbm,
    k_hbm,
    v_hbm,
    out_ref,
    path_ref,
    k_raw,
    v_raw,
    k_wide,
    v_wide,
    q_raw,
    qf,
    q_ref,
    tf,
    p_ref,
    acc_ref,
    sh_ref,
    of,
    pf,
    sem,
    q_sem,
    *,
    kvh,
    groups,
    tree,
    c,
    sub,
    scale,
):
    m = groups * tree
    hd = q_ref.shape[2]
    heads = kvh * groups
    length = lens[0]
    chunks = pl.cdiv(length, c)

    def copies(n, slot):
        span = pl.ds(pl.multiple_of(n * c * kvh, c * kvh), c * kvh)
        return (
            pltpu.make_async_copy(k_hbm.at[span], k_raw.at[slot], sem.at[slot, 0]),
            pltpu.make_async_copy(v_hbm.at[span], v_raw.at[slot], sem.at[slot, 1]),
        )

    def fetch(n, slot):
        @pl.when(n < chunks)
        def _():
            for copy in copies(n, slot):
                copy.start()

    def head_rows(ref, g, start, count):
        return ref[pl.ds(g + kvh * start, count, stride=kvh), :]

    def tree_values(g):
        value = tf[1, pl.ds(g, tree, stride=kvh), :].astype(BF16)
        return jnp.concatenate([value, jnp.ones((tree, hd), BF16)], axis=1)

    def tree_scores(g):
        keys = tf[0, pl.ds(g, tree, stride=kvh), :].astype(BF16)
        return dot_nt(q_ref[g], keys) * scale

    q_copy = pltpu.make_async_copy(q_hbm, q_raw, q_sem)
    q_copy.start()
    fetch(0, 0)
    fetch(1, 1)
    tf[0] = tk_ref[...].astype(F32)
    tf[1] = tv_ref[...].astype(F32)
    allowed = jnp.tile(ancestors(parent_ref[...]), (groups, 1))
    diag_row = lax.broadcasted_iota(jnp.int32, (m, tree), 0) % tree
    diag = diag_row == lax.broadcasted_iota(jnp.int32, (m, tree), 1)
    q_copy.wait()
    qf[...] = q_raw[...].astype(F32)
    for g in range(kvh):
        for h in range(groups):
            part = qf[pl.ds(g * groups + h, tree, stride=heads), :]
            q_ref[g, h * tree : (h + 1) * tree] = part.astype(BF16)
    for g in range(kvh):
        s = tree_scores(g)
        own = jnp.where(diag, s, 0.0).astype(BF16)
        shift = jnp.dot(own, jnp.ones((tree, 128), BF16), preferred_element_type=F32)
        sh_ref[g] = shift
        p = jnp.where(allowed, jnp.exp2(s - shift[:, :tree]), 0.0).astype(BF16)
        acc_ref[g] = jnp.dot(p, tree_values(g), preferred_element_type=F32)

    def widen(raw, wide, slot):
        for i in range(c // sub):
            rows = slice(i * sub * kvh, (i + 1) * sub * kvh)
            wide[rows] = raw[slot, rows].astype(F32)

    def absorb(n, carry):
        slot = lax.rem(n, 2)
        for copy in copies(n, slot):
            copy.wait()
        live = lax.broadcasted_iota(jnp.int32, (c, 128), 0) < length - n * c
        ones = jnp.where(live, 1.0, 0.0).astype(BF16)
        widen(k_raw, k_wide, slot)
        for g in range(kvh):
            q = q_ref[g]
            shift = sh_ref[g]
            for i in range(c // sub):
                s = dot_nt(q, head_rows(k_wide, g, i * sub, sub).astype(BF16))
                p = [jnp.exp2(s[:, a : a + 128] * scale - shift) for a in range(0, sub, 128)]
                p_ref[g % 2, :, i * sub : (i + 1) * sub] = jnp.concatenate(p, axis=1).astype(BF16)
            if g == 0:
                widen(v_raw, v_wide, slot)
            value = jnp.where(live, head_rows(v_wide, g, 0, c), 0.0).astype(BF16)
            value = jnp.concatenate([value, ones], axis=1)
            acc_ref[g] += jnp.dot(p_ref[g % 2], value, preferred_element_type=F32)
        fetch(n + 2, slot)
        return carry

    lax.fori_loop(0, chunks, absorb, 0)

    fits = jnp.max(jnp.where(acc_ref[:, :, hd:] < LIMIT, 0.0, 1.0)) < 0.5

    @pl.when(jnp.logical_not(fits))
    def _():
        again = jnp.tile(ancestors(parent_ref[...]), (groups, 1))
        for g in range(kvh):
            s = jnp.where(again, tree_scores(g), NEG)
            top = jnp.max(s, axis=1, keepdims=True)
            p = jnp.where(again, jnp.exp2(s - top), 0.0).astype(BF16)
            sh_ref[g] = jnp.broadcast_to(top, (m, 128))
            acc_ref[g] = jnp.dot(p, tree_values(g), preferred_element_type=F32)

        def step(i, carry):
            span = pl.ds(pl.multiple_of(i * sub * kvh, sub * kvh), sub * kvh)
            block = pl.ds(0, sub * kvh)
            moves = (
                pltpu.make_async_copy(k_hbm.at[span], k_raw.at[0, block], sem.at[0, 0]),
                pltpu.make_async_copy(v_hbm.at[span], v_raw.at[0, block], sem.at[0, 1]),
            )
            for move in moves:
                move.start()
            for move in moves:
                move.wait()
            k_wide[: sub * kvh] = k_raw[0, : sub * kvh].astype(F32)
            v_wide[: sub * kvh] = v_raw[0, : sub * kvh].astype(F32)
            left = length - i * sub
            col = lax.broadcasted_iota(jnp.int32, (m, sub), 1) < left
            live = lax.broadcasted_iota(jnp.int32, (sub, 128), 0) < left
            ones = jnp.where(live, 1.0, 0.0).astype(BF16)
            for g in range(kvh):
                s = dot_nt(q_ref[g], head_rows(k_wide, g, 0, sub).astype(BF16)) * scale
                s = jnp.where(col, s, NEG)
                old = sh_ref[g]
                top = jnp.maximum(old, jnp.max(s, axis=1, keepdims=True))
                shrink = jnp.exp2(old - top)
                p = [jnp.exp2(s[:, a : a + 128] - top) for a in range(0, sub, 128)]
                p = jnp.concatenate(p, axis=1).astype(BF16)
                value = jnp.where(live, head_rows(v_wide, g, 0, sub), 0.0).astype(BF16)
                value = jnp.concatenate([value, ones], axis=1)
                acc_ref[g] = acc_ref[g] * jnp.concatenate([shrink, shrink], axis=1) + jnp.dot(
                    p, value, preferred_element_type=F32
                )
                sh_ref[g] = top
            return carry

        lax.fori_loop(0, pl.cdiv(length, sub), step, 0)

    for g in range(kvh):
        rows = acc_ref[g, :, :hd] / acc_ref[g, :, hd:]
        for h in range(groups):
            lanes = slice((g * groups + h) * hd, (g * groups + h + 1) * hd)
            part = rows[h * tree : (h + 1) * tree]
            out_ref[:, lanes] = part.astype(BF16)
            of[:, lanes] = part
    for k in range(path_ref.shape[0]):
        row = of[pl.ds(nodes[k], 1), :]
        pf[k : k + 1, :] = jnp.where(k < plen[0], row, 0.0)
    path_ref[...] = pf[...].astype(BF16)


def attention(queries, tree_keys, tree_values, cache_keys, cache_values, lens, parent, nodes, plen):
    tree, heads, hd = queries.shape[1:]
    size, kvh = cache_keys.shape[1:3]
    groups = heads // kvh
    depth = nodes.shape[1]
    m = groups * tree
    c = min(1024, size)
    sub = min(256, c)
    flat = lambda x: x.reshape(-1, hd)
    kernel = functools.partial(
        attention_kernel,
        kvh=kvh,
        groups=groups,
        tree=tree,
        c=c,
        sub=sub,
        scale=math.log2(math.e) / math.sqrt(hd),
    )
    vmem = pl.BlockSpec(memory_space=pltpu.VMEM)
    smem = pl.BlockSpec(memory_space=pltpu.SMEM)
    anywhere = pl.BlockSpec(memory_space=pl.ANY)
    return pl.pallas_call(
        kernel,
        in_specs=[smem, smem, smem, vmem, vmem, vmem, anywhere, anywhere, anywhere],
        out_specs=[vmem, vmem],
        scratch_shapes=[
            pltpu.VMEM((2, c * kvh, hd), BF16),
            pltpu.VMEM((2, c * kvh, hd), BF16),
            pltpu.VMEM((c * kvh, hd), F32),
            pltpu.VMEM((c * kvh, hd), F32),
            pltpu.VMEM((tree * heads, hd), BF16),
            pltpu.VMEM((tree * heads, hd), F32),
            pltpu.VMEM((kvh, m, hd), BF16),
            pltpu.VMEM((2, tree * kvh, hd), F32),
            pltpu.VMEM((2, m, c), BF16),
            pltpu.VMEM((kvh, m, 2 * hd), F32),
            pltpu.VMEM((kvh, m, 128), F32),
            pltpu.VMEM((tree, heads * hd), F32),
            pltpu.VMEM((depth, heads * hd), F32),
            pltpu.SemaphoreType.DMA((2, 2)),
            pltpu.SemaphoreType.DMA(()),
        ],
        out_shape=[
            jax.ShapeDtypeStruct((tree, heads * hd), BF16),
            jax.ShapeDtypeStruct((depth, heads * hd), BF16),
        ],
        name="attention",
    )(
        lens,
        nodes.reshape(-1),
        plen,
        parent,
        flat(tree_keys),
        flat(tree_values),
        flat(queries),
        flat(cache_keys),
        flat(cache_values),
    )


def swap(x, axis, bit):
    size = lax.axis_size(axis)
    return lax.ppermute(x, axis, [(i, i ^ bit) for i in range(size)])


def bits_down(size):
    return [1 << b for b in reversed(range((size - 1).bit_length()))]


def gather_xor(x, axis):
    size = lax.axis_size(axis)
    bits = bits_down(size)
    parts, order = [x], [0]
    if size > 16:
        for bit in bits:
            x = jnp.concatenate([x, swap(x, axis, bit)], axis=0)
            order = order + [b ^ bit for b in order]
        return x, order
    stages = [[bit] for bit in bits]
    if len(bits) > 2:
        stages = [[bits[1], bits[0], bits[0] ^ bits[1]]] + stages[2:]
    for masks in stages:
        parts = parts + [swap(part, axis, mask) for mask in masks for part in parts]
        order = order + [b ^ mask for mask in masks for b in order]
    return jnp.concatenate(parts, axis=0), order


def shards(
    queries,
    tree_keys,
    tree_values,
    cache_keys,
    cache_values,
    cache_len,
    tree_parent,
    path_nodes,
    path_len,
    out_weight,
    norm_gain,
):
    verify, picked = attention(
        queries, tree_keys, tree_values, cache_keys, cache_values, cache_len, tree_parent, path_nodes, path_len
    )
    dp = lax.axis_size("dp")
    tensor = lax.axis_size("tensor")
    depth = path_nodes.shape[1]
    width = dp * out_weight.shape[1]
    rows, order = gather_xor(picked, "dp")
    projected = jnp.dot(rows, out_weight, preferred_element_type=F32)
    position = [0] * dp
    for at, block in enumerate(order):
        position[block] = at
    blocks = jnp.arange(dp, dtype=jnp.int32) ^ lax.axis_index("dp")
    projected = projected.reshape(dp, depth, -1)[jnp.asarray(position, jnp.int32)[blocks]]
    projected = projected.reshape(dp * depth, -1)
    tokens = dp * depth // tensor
    if tensor == 2:
        mine = lax.axis_index("tensor")
        away = lax.dynamic_slice_in_dim(projected, (1 - mine) * tokens, tokens, 0)
        kept = lax.dynamic_slice_in_dim(projected, mine * tokens, tokens, 0)
        summed = kept + swap(away.astype(BF16), "tensor", 1).astype(F32)
    else:
        summed = lax.psum_scatter(projected.astype(BF16), "tensor", tiled=True).astype(F32)
    squares = jnp.sum(summed * summed, axis=1)
    for bit in bits_down(dp):
        squares = squares + swap(squares, "dp", bit)
    inverse = lax.rsqrt(squares / width + EPSILON)
    hidden = summed * inverse[:, None] * norm_gain[None, :]
    return (verify[None], hidden.astype(BF16))


def solution(mesh):
    return jax.shard_map(
        shards,
        mesh=mesh,
        in_specs=(
            P("dp", None, "tensor", None),
            P("dp", None, "tensor", None),
            P("dp", None, "tensor", None),
            P("dp", None, "tensor", None),
            P("dp", None, "tensor", None),
            P("dp"),
            P("dp", None),
            P("dp", None),
            P("dp"),
            P("tensor", "dp"),
            P("dp"),
        ),
        out_specs=(P("dp", None, "tensor"), P("tensor", "dp")),
        check_vma=False,
    )
```

```python
import functools
import math

import jax
import jax.numpy as jnp
from jax import lax
from jax.experimental import pallas as pl
from jax.experimental.pallas import tpu as pltpu
from jax.sharding import PartitionSpec as P

EPSILON = 1e-05
NEG = -1e30
LIMIT = 2.0**100
F32 = jnp.float32
BF16 = jnp.bfloat16


def dot_nt(a, b):
    return lax.dot_general(a, b, (((1,), (1,)), ((), ())), preferred_element_type=F32)


def ancestors(parent_row):
    t = parent_row.shape[1]
    row = lax.broadcasted_iota(jnp.int32, (t, t), 0)
    col = lax.broadcasted_iota(jnp.int32, (t, t), 1)
    reach = jnp.where((parent_row == row) | (row == col), 1.0, 0.0)
    for _ in range(max(1, (t - 1).bit_length())):
        half = reach.astype(BF16)
        reach = jnp.minimum(jnp.dot(half, half, preferred_element_type=F32), 1.0)
    return reach.T > 0.5


def attention_kernel(
    lens_hbm,
    nodes_hbm,
    plen_hbm,
    parent_hbm,
    tk_hbm,
    tv_hbm,
    q_hbm,
    k_hbm,
    v_hbm,
    out_ref,
    path_ref,
    lens,
    nodes,
    plen,
    parent_ref,
    tk_ref,
    tv_ref,
    k_raw,
    v_raw,
    k_wide,
    v_wide,
    q_raw,
    qf,
    q_ref,
    tf,
    p_ref,
    acc_ref,
    sh_ref,
    of,
    pf,
    sem,
    small_sem,
    *,
    kvh,
    groups,
    tree,
    c,
    sub,
    scale,
):
    m = groups * tree
    hd = q_ref.shape[2]
    heads = kvh * groups
    small = [
        pltpu.make_async_copy(source, target, small_sem.at[at])
        for at, (source, target) in enumerate(
            (
                (lens_hbm, lens),
                (parent_hbm, parent_ref),
                (tk_hbm, tk_ref),
                (tv_hbm, tv_ref),
                (q_hbm, q_raw),
                (nodes_hbm, nodes),
                (plen_hbm, plen),
            )
        )
    ]

    def copy_keys(n):
        span = pl.ds(pl.multiple_of(jnp.minimum(n, last) * c * kvh, c * kvh), c * kvh)
        slot = lax.rem(n, 2)
        return pltpu.make_async_copy(k_hbm.at[span], k_raw.at[slot], sem.at[0, slot])

    def copy_values(n):
        span = pl.ds(pl.multiple_of(jnp.minimum(n, last) * c * kvh, c * kvh), c * kvh)
        slot = lax.rem(n, 2)
        return pltpu.make_async_copy(v_hbm.at[span], v_raw.at[slot], sem.at[1, slot])

    for copy in small[:5]:
        copy.start()
    head = pl.ds(0, c * kvh)
    pltpu.make_async_copy(k_hbm.at[head], k_raw.at[0], sem.at[0, 0]).start()
    pltpu.make_async_copy(v_hbm.at[head], v_raw.at[0], sem.at[1, 0]).start()
    small[0].wait()
    length = lens[0]
    chunks = pl.cdiv(length, c)
    last = chunks - 1
    copy_keys(1).start()
    for copy in small[5:]:
        copy.start()

    def head_rows(ref, g, start, count):
        return ref[pl.ds(g + kvh * start, count, stride=kvh), :]

    def tree_values(g):
        value = tf[1, pl.ds(g, tree, stride=kvh), :].astype(BF16)
        return jnp.concatenate([value, jnp.ones((tree, hd), BF16)], axis=1)

    def tree_scores(g):
        keys = tf[0, pl.ds(g, tree, stride=kvh), :].astype(BF16)
        return dot_nt(q_ref[g], keys) * scale

    def widen(raw, wide):
        for i in range(c // sub):
            rows = slice(i * sub * kvh, (i + 1) * sub * kvh)
            wide[rows] = raw[rows].astype(F32)

    for copy in small[1:4]:
        copy.wait()
    tf[0] = tk_ref[...].astype(F32)
    tf[1] = tv_ref[...].astype(F32)
    allowed = jnp.tile(ancestors(parent_ref[...]), (groups, 1))
    diag_row = lax.broadcasted_iota(jnp.int32, (m, tree), 0) % tree
    diag = diag_row == lax.broadcasted_iota(jnp.int32, (m, tree), 1)
    small[4].wait()
    copy_keys(0).wait()
    widen(k_raw.at[0], k_wide)
    qf[...] = q_raw[...].astype(F32)
    for g in range(kvh):
        for h in range(groups):
            part = qf[pl.ds(g * groups + h, tree, stride=heads), :]
            q_ref[g, h * tree : (h + 1) * tree] = part.astype(BF16)
    for g in range(kvh):
        s = tree_scores(g)
        own = jnp.where(diag, s, 0.0).astype(BF16)
        shift = jnp.dot(own, jnp.ones((tree, 128), BF16), preferred_element_type=F32)
        sh_ref[g] = shift
        p = jnp.where(allowed, jnp.exp2(s - shift[:, :tree]), 0.0).astype(BF16)
        acc_ref[g] = jnp.dot(p, tree_values(g), preferred_element_type=F32)

    def absorb(n, carry):
        slot = lax.rem(n, 2)
        copy_keys(n + 1).wait()
        copy_values(n).wait()
        copy_keys(n + 2).start()
        copy_values(n + 1).start()
        live = lax.broadcasted_iota(jnp.int32, (c, 128), 0) < length - n * c
        ones = jnp.where(live, 1.0, 0.0).astype(BF16)
        for g in range(kvh):
            q = q_ref[g]
            shift = sh_ref[g]
            for i in range(c // sub):
                s = dot_nt(q, head_rows(k_wide, g, i * sub, sub).astype(BF16))
                p = [jnp.exp2(s[:, a : a + 128] * scale - shift) for a in range(0, sub, 128)]
                p_ref[g % 2, :, i * sub : (i + 1) * sub] = jnp.concatenate(p, axis=1).astype(BF16)
            if g == 0:
                widen(v_raw.at[slot], v_wide)
            if g == kvh - 1:
                widen(k_raw.at[1 - slot], k_wide)
            value = jnp.where(live, head_rows(v_wide, g, 0, c), 0.0).astype(BF16)
            value = jnp.concatenate([value, ones], axis=1)
            acc_ref[g] += jnp.dot(p_ref[g % 2], value, preferred_element_type=F32)
        return carry

    lax.fori_loop(0, chunks, absorb, 0)
    copy_keys(chunks + 1).wait()
    copy_values(chunks).wait()

    fits = jnp.max(jnp.where(acc_ref[:, :, hd:] < LIMIT, 0.0, 1.0)) < 0.5

    @pl.when(jnp.logical_not(fits))
    def _():
        again = jnp.tile(ancestors(parent_ref[...]), (groups, 1))
        for g in range(kvh):
            s = jnp.where(again, tree_scores(g), NEG)
            top = jnp.max(s, axis=1, keepdims=True)
            p = jnp.where(again, jnp.exp2(s - top), 0.0).astype(BF16)
            sh_ref[g] = jnp.broadcast_to(top, (m, 128))
            acc_ref[g] = jnp.dot(p, tree_values(g), preferred_element_type=F32)

        def step(i, carry):
            span = pl.ds(pl.multiple_of(i * sub * kvh, sub * kvh), sub * kvh)
            block = pl.ds(0, sub * kvh)
            moves = (
                pltpu.make_async_copy(k_hbm.at[span], k_raw.at[0, block], sem.at[0, 0]),
                pltpu.make_async_copy(v_hbm.at[span], v_raw.at[0, block], sem.at[1, 0]),
            )
            for move in moves:
                move.start()
            for move in moves:
                move.wait()
            k_wide[: sub * kvh] = k_raw[0, : sub * kvh].astype(F32)
            v_wide[: sub * kvh] = v_raw[0, : sub * kvh].astype(F32)
            left = length - i * sub
            col = lax.broadcasted_iota(jnp.int32, (m, sub), 1) < left
            live = lax.broadcasted_iota(jnp.int32, (sub, 128), 0) < left
            ones = jnp.where(live, 1.0, 0.0).astype(BF16)
            for g in range(kvh):
                s = dot_nt(q_ref[g], head_rows(k_wide, g, 0, sub).astype(BF16)) * scale
                s = jnp.where(col, s, NEG)
                old = sh_ref[g]
                top = jnp.maximum(old, jnp.max(s, axis=1, keepdims=True))
                shrink = jnp.exp2(old - top)
                p = [jnp.exp2(s[:, a : a + 128] - top) for a in range(0, sub, 128)]
                p = jnp.concatenate(p, axis=1).astype(BF16)
                value = jnp.where(live, head_rows(v_wide, g, 0, sub), 0.0).astype(BF16)
                value = jnp.concatenate([value, ones], axis=1)
                acc_ref[g] = acc_ref[g] * jnp.concatenate([shrink, shrink], axis=1) + jnp.dot(
                    p, value, preferred_element_type=F32
                )
                sh_ref[g] = top
            return carry

        lax.fori_loop(0, pl.cdiv(length, sub), step, 0)

    for g in range(kvh):
        rows = acc_ref[g, :, :hd] / acc_ref[g, :, hd:]
        for h in range(groups):
            lanes = slice((g * groups + h) * hd, (g * groups + h + 1) * hd)
            part = rows[h * tree : (h + 1) * tree]
            out_ref[:, lanes] = part.astype(BF16)
            of[:, lanes] = part
    for copy in small[5:]:
        copy.wait()
    for k in range(path_ref.shape[0]):
        row = of[pl.ds(nodes[0, k], 1), :]
        pf[k : k + 1, :] = jnp.where(k < plen[0], row, 0.0)
    path_ref[...] = pf[...].astype(BF16)


def attention(queries, tree_keys, tree_values, cache_keys, cache_values, lens, parent, nodes, plen):
    tree, heads, hd = queries.shape[1:]
    size, kvh = cache_keys.shape[1:3]
    groups = heads // kvh
    depth = nodes.shape[1]
    m = groups * tree
    c = min(2048, size)
    sub = min(256, c)
    flat = lambda x: x.reshape(-1, hd)
    kernel = functools.partial(
        attention_kernel,
        kvh=kvh,
        groups=groups,
        tree=tree,
        c=c,
        sub=sub,
        scale=math.log2(math.e) / math.sqrt(hd),
    )
    vmem = pl.BlockSpec(memory_space=pltpu.VMEM)
    anywhere = pl.BlockSpec(memory_space=pltpu.HBM)
    return pl.pallas_call(
        kernel,
        in_specs=[anywhere] * 9,
        out_specs=[vmem, vmem],
        scratch_shapes=[
            pltpu.SMEM((1,), jnp.int32),
            pltpu.SMEM((1, depth), jnp.int32),
            pltpu.SMEM((1,), jnp.int32),
            pltpu.VMEM((1, tree), jnp.int32),
            pltpu.VMEM((tree * kvh, hd), BF16),
            pltpu.VMEM((tree * kvh, hd), BF16),
            pltpu.VMEM((2, c * kvh, hd), BF16),
            pltpu.VMEM((2, c * kvh, hd), BF16),
            pltpu.VMEM((c * kvh, hd), F32),
            pltpu.VMEM((c * kvh, hd), F32),
            pltpu.VMEM((tree * heads, hd), BF16),
            pltpu.VMEM((tree * heads, hd), F32),
            pltpu.VMEM((kvh, m, hd), BF16),
            pltpu.VMEM((2, tree * kvh, hd), F32),
            pltpu.VMEM((2, m, c), BF16),
            pltpu.VMEM((kvh, m, 2 * hd), F32),
            pltpu.VMEM((kvh, m, 128), F32),
            pltpu.VMEM((tree, heads * hd), F32),
            pltpu.VMEM((depth, heads * hd), F32),
            pltpu.SemaphoreType.DMA((2, 2)),
            pltpu.SemaphoreType.DMA((7,)),
        ],
        out_shape=[
            jax.ShapeDtypeStruct((tree, heads * hd), BF16),
            jax.ShapeDtypeStruct((depth, heads * hd), BF16),
        ],
        name="attention",
    )(
        lens,
        nodes,
        plen,
        parent,
        flat(tree_keys),
        flat(tree_values),
        flat(queries),
        flat(cache_keys),
        flat(cache_values),
    )


def swap(x, axis, bit):
    size = lax.axis_size(axis)
    return lax.ppermute(x, axis, [(i, i ^ bit) for i in range(size)])


def bits_down(size):
    return [1 << b for b in reversed(range((size - 1).bit_length()))]


def gather_xor(x, axis):
    size = lax.axis_size(axis)
    bits = bits_down(size)
    parts, order = [x], [0]
    if size > 16:
        for bit in bits:
            x = jnp.concatenate([x, swap(x, axis, bit)], axis=0)
            order = order + [b ^ bit for b in order]
        return x, order
    stages = [[bit] for bit in bits]
    if len(bits) > 2:
        stages = [[bits[0], bits[1], bits[0] ^ bits[1]]] + stages[2:]
    for masks in stages:
        parts = parts + [swap(part, axis, mask) for mask in masks for part in parts]
        order = order + [b ^ mask for mask in masks for b in order]
    return jnp.concatenate(parts, axis=0), order


def shards(
    queries,
    tree_keys,
    tree_values,
    cache_keys,
    cache_values,
    cache_len,
    tree_parent,
    path_nodes,
    path_len,
    out_weight,
    norm_gain,
):
    verify, picked = attention(
        queries, tree_keys, tree_values, cache_keys, cache_values, cache_len, tree_parent, path_nodes, path_len
    )
    dp = lax.axis_size("dp")
    tensor = lax.axis_size("tensor")
    depth = path_nodes.shape[1]
    width = dp * out_weight.shape[1]
    rows, order = gather_xor(picked, "dp")
    projected = jnp.dot(rows, out_weight, preferred_element_type=F32)
    position = [0] * dp
    for at, block in enumerate(order):
        position[block] = at
    blocks = jnp.arange(dp, dtype=jnp.int32) ^ lax.axis_index("dp")
    projected = projected.reshape(dp, depth, -1)[jnp.asarray(position, jnp.int32)[blocks]]
    projected = projected.reshape(dp * depth, -1)
    tokens = dp * depth // tensor
    if tensor == 2:
        mine = lax.axis_index("tensor")
        away = lax.dynamic_slice_in_dim(projected, (1 - mine) * tokens, tokens, 0)
        kept = lax.dynamic_slice_in_dim(projected, mine * tokens, tokens, 0)
        summed = kept + swap(away.astype(BF16), "tensor", 1).astype(F32)
    else:
        summed = lax.psum_scatter(projected.astype(BF16), "tensor", tiled=True).astype(F32)
    squares = jnp.sum(summed * summed, axis=1)
    for bit in bits_down(dp):
        squares = squares + swap(squares, "dp", bit)
    inverse = lax.rsqrt(squares / width + EPSILON)
    hidden = summed * inverse[:, None] * norm_gain[None, :]
    return (verify[None], hidden.astype(BF16))


def solution(mesh):
    return jax.shard_map(
        shards,
        mesh=mesh,
        in_specs=(
            P("dp", None, "tensor", None),
            P("dp", None, "tensor", None),
            P("dp", None, "tensor", None),
            P("dp", None, "tensor", None),
            P("dp", None, "tensor", None),
            P("dp"),
            P("dp", None),
            P("dp", None),
            P("dp"),
            P("tensor", "dp"),
            P("dp"),
        ),
        out_specs=(P("dp", None, "tensor"), P("tensor", "dp")),
        check_vma=False,
    )
```

```python
import functools
import math

import jax
import jax.numpy as jnp
from jax import lax
from jax.experimental import pallas as pl
from jax.experimental.pallas import tpu as pltpu
from jax.sharding import PartitionSpec as P

EPSILON = 1e-05
NEG = -1e30
LIMIT = 2.0**100
F32 = jnp.float32
BF16 = jnp.bfloat16


def dot_nt(a, b):
    return lax.dot_general(a, b, (((1,), (1,)), ((), ())), preferred_element_type=F32)


def ancestors(parent_row):
    t = parent_row.shape[1]
    row = lax.broadcasted_iota(jnp.int32, (t, t), 0)
    col = lax.broadcasted_iota(jnp.int32, (t, t), 1)
    reach = jnp.where((parent_row == row) | (row == col), 1.0, 0.0)
    for _ in range(max(1, (t - 1).bit_length())):
        half = reach.astype(BF16)
        reach = jnp.minimum(jnp.dot(half, half, preferred_element_type=F32), 1.0)
    return reach.T > 0.5


def attention_kernel(
    lens_hbm,
    nodes_hbm,
    plen_hbm,
    parent_hbm,
    tk_hbm,
    tv_hbm,
    q_hbm,
    k_hbm,
    v_hbm,
    out_ref,
    path_ref,
    lens,
    nodes,
    plen,
    parent_ref,
    tk_ref,
    tv_ref,
    k_raw,
    v_raw,
    k_wide,
    v_wide,
    q_raw,
    qf,
    q_ref,
    tf,
    p_ref,
    acc_ref,
    sh_ref,
    of,
    pf,
    sem,
    small_sem,
    *,
    kvh,
    groups,
    tree,
    c,
    sub,
    scale,
):
    m = groups * tree
    hd = q_ref.shape[2]
    heads = kvh * groups
    small = [
        pltpu.make_async_copy(source, target, small_sem.at[at])
        for at, (source, target) in enumerate(
            (
                (lens_hbm, lens),
                (parent_hbm, parent_ref),
                (tk_hbm, tk_ref),
                (tv_hbm, tv_ref),
                (q_hbm, q_raw),
                (nodes_hbm, nodes),
                (plen_hbm, plen),
            )
        )
    ]

    def copy_keys(n):
        span = pl.ds(pl.multiple_of(jnp.minimum(n, last) * c * kvh, c * kvh), c * kvh)
        slot = lax.rem(n, 2)
        return pltpu.make_async_copy(k_hbm.at[span], k_raw.at[slot], sem.at[0, slot])

    def copy_values(n):
        span = pl.ds(pl.multiple_of(jnp.minimum(n, last) * c * kvh, c * kvh), c * kvh)
        slot = lax.rem(n, 2)
        return pltpu.make_async_copy(v_hbm.at[span], v_raw.at[slot], sem.at[1, slot])

    for copy in small[:5]:
        copy.start()
    head = pl.ds(0, c * kvh)
    pltpu.make_async_copy(k_hbm.at[head], k_raw.at[0], sem.at[0, 0]).start()
    pltpu.make_async_copy(v_hbm.at[head], v_raw.at[0], sem.at[1, 0]).start()
    small[0].wait()
    length = lens[0]
    chunks = pl.cdiv(length, c)
    last = chunks - 1
    copy_keys(1).start()
    for copy in small[5:]:
        copy.start()

    def head_rows(ref, g, start, count):
        return ref[pl.ds(g + kvh * start, count, stride=kvh), :]

    def tree_values(g):
        value = tf[1, pl.ds(g, tree, stride=kvh), :].astype(BF16)
        return jnp.concatenate([value, jnp.ones((tree, hd), BF16)], axis=1)

    def tree_scores(g):
        keys = tf[0, pl.ds(g, tree, stride=kvh), :].astype(BF16)
        return dot_nt(q_ref[g], keys) * scale

    def widen(raw, wide):
        for i in range(c // sub):
            rows = slice(i * sub * kvh, (i + 1) * sub * kvh)
            wide[rows] = raw[rows].astype(F32)

    for copy in small[1:4]:
        copy.wait()
    tf[0] = tk_ref[...].astype(F32)
    tf[1] = tv_ref[...].astype(F32)
    allowed = jnp.tile(ancestors(parent_ref[...]), (groups, 1))
    diag_row = lax.broadcasted_iota(jnp.int32, (m, tree), 0) % tree
    diag = diag_row == lax.broadcasted_iota(jnp.int32, (m, tree), 1)
    small[4].wait()
    copy_keys(0).wait()
    widen(k_raw.at[0], k_wide)
    qf[...] = q_raw[...].astype(F32)
    for g in range(kvh):
        for h in range(groups):
            part = qf[pl.ds(g * groups + h, tree, stride=heads), :]
            q_ref[g, h * tree : (h + 1) * tree] = part.astype(BF16)
    for g in range(kvh):
        s = tree_scores(g)
        own = jnp.where(diag, s, 0.0).astype(BF16)
        shift = jnp.dot(own, jnp.ones((tree, 128), BF16), preferred_element_type=F32)
        sh_ref[g] = shift
        p = jnp.where(allowed, jnp.exp2(s - shift[:, :tree]), 0.0).astype(BF16)
        acc_ref[g] = jnp.dot(p, tree_values(g), preferred_element_type=F32)

    def absorb(n, carry):
        slot = lax.rem(n, 2)
        copy_keys(n + 1).wait()
        copy_values(n).wait()
        copy_keys(n + 2).start()
        copy_values(n + 1).start()
        live = lax.broadcasted_iota(jnp.int32, (c, 128), 0) < length - n * c
        ones = jnp.where(live, 1.0, 0.0).astype(BF16)
        for g in range(kvh):
            q = q_ref[g]
            shift = sh_ref[g]
            for i in range(c // sub):
                s = dot_nt(q, head_rows(k_wide, g, i * sub, sub).astype(BF16))
                p = [jnp.exp2(s[:, a : a + 128] * scale - shift) for a in range(0, sub, 128)]
                p_ref[g % 2, :, i * sub : (i + 1) * sub] = jnp.concatenate(p, axis=1).astype(BF16)
            if g == 0:
                widen(v_raw.at[slot], v_wide)
            if g == kvh - 1:
                widen(k_raw.at[1 - slot], k_wide)
            value = jnp.where(live, head_rows(v_wide, g, 0, c), 0.0).astype(BF16)
            value = jnp.concatenate([value, ones], axis=1)
            acc_ref[g] += jnp.dot(p_ref[g % 2], value, preferred_element_type=F32)
        return carry

    lax.fori_loop(0, chunks, absorb, 0)
    copy_keys(chunks + 1).wait()
    copy_values(chunks).wait()

    fits = jnp.max(jnp.where(acc_ref[:, :, hd:] < LIMIT, 0.0, 1.0)) < 0.5

    @pl.when(jnp.logical_not(fits))
    def _():
        again = jnp.tile(ancestors(parent_ref[...]), (groups, 1))
        for g in range(kvh):
            s = jnp.where(again, tree_scores(g), NEG)
            top = jnp.max(s, axis=1, keepdims=True)
            p = jnp.where(again, jnp.exp2(s - top), 0.0).astype(BF16)
            sh_ref[g] = jnp.broadcast_to(top, (m, 128))
            acc_ref[g] = jnp.dot(p, tree_values(g), preferred_element_type=F32)

        def step(i, carry):
            span = pl.ds(pl.multiple_of(i * sub * kvh, sub * kvh), sub * kvh)
            block = pl.ds(0, sub * kvh)
            moves = (
                pltpu.make_async_copy(k_hbm.at[span], k_raw.at[0, block], sem.at[0, 0]),
                pltpu.make_async_copy(v_hbm.at[span], v_raw.at[0, block], sem.at[1, 0]),
            )
            for move in moves:
                move.start()
            for move in moves:
                move.wait()
            k_wide[: sub * kvh] = k_raw[0, : sub * kvh].astype(F32)
            v_wide[: sub * kvh] = v_raw[0, : sub * kvh].astype(F32)
            left = length - i * sub
            col = lax.broadcasted_iota(jnp.int32, (m, sub), 1) < left
            live = lax.broadcasted_iota(jnp.int32, (sub, 128), 0) < left
            ones = jnp.where(live, 1.0, 0.0).astype(BF16)
            for g in range(kvh):
                s = dot_nt(q_ref[g], head_rows(k_wide, g, 0, sub).astype(BF16)) * scale
                s = jnp.where(col, s, NEG)
                old = sh_ref[g]
                top = jnp.maximum(old, jnp.max(s, axis=1, keepdims=True))
                shrink = jnp.exp2(old - top)
                p = [jnp.exp2(s[:, a : a + 128] - top) for a in range(0, sub, 128)]
                p = jnp.concatenate(p, axis=1).astype(BF16)
                value = jnp.where(live, head_rows(v_wide, g, 0, sub), 0.0).astype(BF16)
                value = jnp.concatenate([value, ones], axis=1)
                acc_ref[g] = acc_ref[g] * jnp.concatenate([shrink, shrink], axis=1) + jnp.dot(
                    p, value, preferred_element_type=F32
                )
                sh_ref[g] = top
            return carry

        lax.fori_loop(0, pl.cdiv(length, sub), step, 0)

    for g in range(kvh):
        rows = acc_ref[g, :, :hd] / acc_ref[g, :, hd:]
        for h in range(groups):
            lanes = slice((g * groups + h) * hd, (g * groups + h + 1) * hd)
            part = rows[h * tree : (h + 1) * tree]
            out_ref[:, lanes] = part.astype(BF16)
            of[:, lanes] = part
    for copy in small[5:]:
        copy.wait()
    for k in range(path_ref.shape[0]):
        row = of[pl.ds(nodes[0, k], 1), :]
        pf[k : k + 1, :] = jnp.where(k < plen[0], row, 0.0)
    path_ref[...] = pf[...].astype(BF16)


def attention(queries, tree_keys, tree_values, cache_keys, cache_values, lens, parent, nodes, plen):
    tree, heads, hd = queries.shape[1:]
    size, kvh = cache_keys.shape[1:3]
    groups = heads // kvh
    depth = nodes.shape[1]
    m = groups * tree
    c = min(2048, size)
    sub = min(256, c)
    flat = lambda x: x.reshape(-1, hd)
    kernel = functools.partial(
        attention_kernel,
        kvh=kvh,
        groups=groups,
        tree=tree,
        c=c,
        sub=sub,
        scale=math.log2(math.e) / math.sqrt(hd),
    )
    vmem = pl.BlockSpec(memory_space=pltpu.VMEM)
    anywhere = pl.BlockSpec(memory_space=pltpu.HBM)
    return pl.pallas_call(
        kernel,
        in_specs=[anywhere] * 9,
        out_specs=[vmem, vmem],
        scratch_shapes=[
            pltpu.SMEM((1,), jnp.int32),
            pltpu.SMEM((1, depth), jnp.int32),
            pltpu.SMEM((1,), jnp.int32),
            pltpu.VMEM((1, tree), jnp.int32),
            pltpu.VMEM((tree * kvh, hd), BF16),
            pltpu.VMEM((tree * kvh, hd), BF16),
            pltpu.VMEM((2, c * kvh, hd), BF16),
            pltpu.VMEM((2, c * kvh, hd), BF16),
            pltpu.VMEM((c * kvh, hd), F32),
            pltpu.VMEM((c * kvh, hd), F32),
            pltpu.VMEM((tree * heads, hd), BF16),
            pltpu.VMEM((tree * heads, hd), F32),
            pltpu.VMEM((kvh, m, hd), BF16),
            pltpu.VMEM((2, tree * kvh, hd), F32),
            pltpu.VMEM((2, m, c), BF16),
            pltpu.VMEM((kvh, m, 2 * hd), F32),
            pltpu.VMEM((kvh, m, 128), F32),
            pltpu.VMEM((tree, heads * hd), F32),
            pltpu.VMEM((depth, heads * hd), F32),
            pltpu.SemaphoreType.DMA((2, 2)),
            pltpu.SemaphoreType.DMA((7,)),
        ],
        out_shape=[
            jax.ShapeDtypeStruct((tree, heads * hd), BF16),
            jax.ShapeDtypeStruct((depth, heads * hd), BF16),
        ],
        name="attention",
    )(
        lens,
        nodes,
        plen,
        parent,
        flat(tree_keys),
        flat(tree_values),
        flat(queries),
        flat(cache_keys),
        flat(cache_values),
    )


def swap(x, axis, bit):
    size = lax.axis_size(axis)
    return lax.ppermute(x, axis, [(i, i ^ bit) for i in range(size)])


def bits_down(size):
    return [1 << b for b in reversed(range((size - 1).bit_length()))]


def gather_xor(x, axis):
    size = lax.axis_size(axis)
    bits = bits_down(size)
    parts, order = [x], [0]
    if size > 16:
        for bit in bits:
            x = jnp.concatenate([x, swap(x, axis, bit)], axis=0)
            order = order + [b ^ bit for b in order]
        return [x], order
    stages = [[bit] for bit in bits]
    if len(bits) > 2:
        stages = [[bits[0], bits[1], bits[0] ^ bits[1]]] + stages[2:]
    for masks in stages:
        parts = parts + [swap(part, axis, mask) for mask in masks for part in parts]
        order = order + [b ^ mask for mask in masks for b in order]
    return parts, order


def project_kernel(place, *refs, order, parts, depth, mine_tokens):
    blocks = refs[:parts]
    weight, kept_ref, away_ref, rows, whole = refs[parts:]
    for at in range(parts):
        rows[at * depth : (at + 1) * depth] = blocks[at][...]
    total = jnp.dot(rows[...], weight[...], preferred_element_type=F32)
    for at, block in enumerate(order):
        row = jnp.bitwise_xor(place[0], block) * depth
        whole[pl.ds(pl.multiple_of(row, depth), depth)] = total[at * depth : (at + 1) * depth]
    kept = pl.multiple_of(place[1] * mine_tokens, mine_tokens)
    away = pl.multiple_of((1 - place[1]) * mine_tokens, mine_tokens)
    kept_ref[...] = whole[pl.ds(kept, mine_tokens)]
    away_ref[...] = whole[pl.ds(away, mine_tokens)].astype(BF16)


def project_halves(parts, order, weight, mine_tokens):
    depth, inputs = parts[0].shape
    columns = weight.shape[1]
    place = jnp.stack([lax.axis_index("dp"), lax.axis_index("tensor")]).astype(jnp.int32)
    vmem = pl.BlockSpec(memory_space=pltpu.VMEM)
    return pl.pallas_call(
        functools.partial(
            project_kernel, order=order, parts=len(parts), depth=depth, mine_tokens=mine_tokens
        ),
        in_specs=[pl.BlockSpec(memory_space=pltpu.SMEM)]
        + [vmem] * (len(parts) + 1),
        out_specs=[vmem, vmem],
        scratch_shapes=[
            pltpu.VMEM((depth * len(parts), inputs), BF16),
            pltpu.VMEM((depth * len(parts), columns), F32),
        ],
        out_shape=[
            jax.ShapeDtypeStruct((mine_tokens, columns), F32),
            jax.ShapeDtypeStruct((mine_tokens, columns), BF16),
        ],
        compiler_params=pltpu.CompilerParams(vmem_limit_bytes=16 * 2**20),
        name="project",
    )(place, *parts, weight)


def shards(
    queries,
    tree_keys,
    tree_values,
    cache_keys,
    cache_values,
    cache_len,
    tree_parent,
    path_nodes,
    path_len,
    out_weight,
    norm_gain,
):
    verify, picked = attention(
        queries, tree_keys, tree_values, cache_keys, cache_values, cache_len, tree_parent, path_nodes, path_len
    )
    dp = lax.axis_size("dp")
    tensor = lax.axis_size("tensor")
    depth = path_nodes.shape[1]
    width = dp * out_weight.shape[1]
    parts, order = gather_xor(picked, "dp")
    tokens = dp * depth // tensor
    if tensor == 2 and len(parts) == dp:
        kept, away = project_halves(parts, order, out_weight, tokens)
        summed = kept + swap(away, "tensor", 1).astype(F32)
    else:
        rows = jnp.concatenate(parts, axis=0)
        projected = jnp.dot(rows, out_weight, preferred_element_type=F32)
        position = [0] * dp
        for at, block in enumerate(order):
            position[block] = at
        blocks = jnp.arange(dp, dtype=jnp.int32) ^ lax.axis_index("dp")
        projected = projected.reshape(dp, depth, -1)[jnp.asarray(position, jnp.int32)[blocks]]
        projected = projected.reshape(dp * depth, -1)
        summed = lax.psum_scatter(projected.astype(BF16), "tensor", tiled=True).astype(F32)
    squares = jnp.sum(summed * summed, axis=1)
    for bit in bits_down(dp):
        squares = squares + swap(squares, "dp", bit)
    inverse = lax.rsqrt(squares / width + EPSILON)
    hidden = summed * inverse[:, None] * norm_gain[None, :]
    return (verify[None], hidden.astype(BF16))


def solution(mesh):
    return jax.shard_map(
        shards,
        mesh=mesh,
        in_specs=(
            P("dp", None, "tensor", None),
            P("dp", None, "tensor", None),
            P("dp", None, "tensor", None),
            P("dp", None, "tensor", None),
            P("dp", None, "tensor", None),
            P("dp"),
            P("dp", None),
            P("dp", None),
            P("dp"),
            P("tensor", "dp"),
            P("dp"),
        ),
        out_specs=(P("dp", None, "tensor"), P("tensor", "dp")),
        check_vma=False,
    )
```

```python
import functools
import math

import jax
import jax.numpy as jnp
from jax import lax
from jax.experimental import pallas as pl
from jax.experimental.pallas import tpu as pltpu
from jax.sharding import PartitionSpec as P

EPSILON = 1e-05
NEG = -1e30
LIMIT = 2.0**100
F32 = jnp.float32
BF16 = jnp.bfloat16


def dot_nt(a, b):
    return lax.dot_general(a, b, (((1,), (1,)), ((), ())), preferred_element_type=F32)


def ancestors(parent_row):
    t = parent_row.shape[1]
    row = lax.broadcasted_iota(jnp.int32, (t, t), 0)
    col = lax.broadcasted_iota(jnp.int32, (t, t), 1)
    reach = jnp.where((parent_row == row) | (row == col), 1.0, 0.0)
    for _ in range(max(1, (t - 1).bit_length())):
        half = reach.astype(BF16)
        reach = jnp.minimum(jnp.dot(half, half, preferred_element_type=F32), 1.0)
    return reach.T > 0.5


def attention_kernel(
    lens_hbm,
    nodes_hbm,
    plen_hbm,
    parent_hbm,
    tk_hbm,
    tv_hbm,
    q_hbm,
    k_hbm,
    v_hbm,
    out_ref,
    path_ref,
    lens,
    nodes,
    plen,
    parent_ref,
    tk_ref,
    tv_ref,
    k_raw,
    v_raw,
    k_wide,
    v_wide,
    q_raw,
    qf,
    q_ref,
    tf,
    p_ref,
    acc_ref,
    sh_ref,
    of,
    pf,
    sem,
    small_sem,
    *,
    kvh,
    groups,
    tree,
    c,
    sub,
    scale,
):
    m = groups * tree
    hd = q_ref.shape[2]
    heads = kvh * groups
    small = [
        pltpu.make_async_copy(source, target, small_sem.at[at])
        for at, (source, target) in enumerate(
            (
                (lens_hbm, lens),
                (parent_hbm, parent_ref),
                (tk_hbm, tk_ref),
                (tv_hbm, tv_ref),
                (q_hbm, q_raw),
                (nodes_hbm, nodes),
                (plen_hbm, plen),
            )
        )
    ]

    def copy_keys(n):
        span = pl.ds(pl.multiple_of(jnp.minimum(n, last) * c * kvh, c * kvh), c * kvh)
        slot = lax.rem(n, 2)
        return pltpu.make_async_copy(k_hbm.at[span], k_raw.at[slot], sem.at[0, slot])

    def copy_values(n):
        span = pl.ds(pl.multiple_of(jnp.minimum(n, last) * c * kvh, c * kvh), c * kvh)
        slot = lax.rem(n, 2)
        return pltpu.make_async_copy(v_hbm.at[span], v_raw.at[slot], sem.at[1, slot])

    for copy in small[:5]:
        copy.start()
    head = pl.ds(0, c * kvh)
    pltpu.make_async_copy(k_hbm.at[head], k_raw.at[0], sem.at[0, 0]).start()
    pltpu.make_async_copy(v_hbm.at[head], v_raw.at[0], sem.at[1, 0]).start()
    small[0].wait()
    length = lens[0]
    chunks = pl.cdiv(length, c)
    last = chunks - 1
    copy_keys(1).start()
    for copy in small[5:]:
        copy.start()

    def head_rows(ref, g, start, count):
        return ref[pl.ds(g + kvh * start, count, stride=kvh), :]

    def tree_values(g):
        value = tf[1, pl.ds(g, tree, stride=kvh), :].astype(BF16)
        return jnp.concatenate([value, jnp.ones((tree, hd), BF16)], axis=1)

    def tree_scores(g):
        keys = tf[0, pl.ds(g, tree, stride=kvh), :].astype(BF16)
        return dot_nt(q_ref[g], keys) * scale

    def widen(raw, wide):
        for i in range(c // sub):
            rows = slice(i * sub * kvh, (i + 1) * sub * kvh)
            wide[rows] = raw[rows].astype(F32)

    for copy in small[1:4]:
        copy.wait()
    tf[0] = tk_ref[...].astype(F32)
    tf[1] = tv_ref[...].astype(F32)
    allowed = jnp.tile(ancestors(parent_ref[...]), (groups, 1))
    diag_row = lax.broadcasted_iota(jnp.int32, (m, tree), 0) % tree
    diag = diag_row == lax.broadcasted_iota(jnp.int32, (m, tree), 1)
    small[4].wait()
    copy_keys(0).wait()
    widen(k_raw.at[0], k_wide)
    qf[...] = q_raw[...].astype(F32)
    for g in range(kvh):
        for h in range(groups):
            part = qf[pl.ds(g * groups + h, tree, stride=heads), :]
            q_ref[g, h * tree : (h + 1) * tree] = part.astype(BF16)
    for g in range(kvh):
        s = tree_scores(g)
        own = jnp.where(diag, s, 0.0).astype(BF16)
        shift = jnp.dot(own, jnp.ones((tree, 128), BF16), preferred_element_type=F32)
        sh_ref[g] = shift
        p = jnp.where(allowed, jnp.exp2(s - shift[:, :tree]), 0.0).astype(BF16)
        acc_ref[g] = jnp.dot(p, tree_values(g), preferred_element_type=F32)

    def absorb(n, carry):
        slot = lax.rem(n, 2)
        copy_keys(n + 1).wait()
        copy_values(n).wait()
        copy_keys(n + 2).start()
        copy_values(n + 1).start()
        live = lax.broadcasted_iota(jnp.int32, (c, 128), 0) < length - n * c
        ones = jnp.where(live, 1.0, 0.0).astype(BF16)
        for g in range(kvh):
            q = q_ref[g]
            shift = sh_ref[g]
            for i in range(c // sub):
                s = dot_nt(q, head_rows(k_wide, g, i * sub, sub).astype(BF16))
                p = [jnp.exp2(s[:, a : a + 128] * scale - shift) for a in range(0, sub, 128)]
                p_ref[g % 2, :, i * sub : (i + 1) * sub] = jnp.concatenate(p, axis=1).astype(BF16)
            if g == 0:
                widen(v_raw.at[slot], v_wide)
            if g == kvh - 1:
                widen(k_raw.at[1 - slot], k_wide)
            value = jnp.where(live, head_rows(v_wide, g, 0, c), 0.0).astype(BF16)
            value = jnp.concatenate([value, ones], axis=1)
            acc_ref[g] += jnp.dot(p_ref[g % 2], value, preferred_element_type=F32)
        return carry

    lax.fori_loop(0, chunks, absorb, 0)
    copy_keys(chunks + 1).wait()
    copy_values(chunks).wait()

    fits = jnp.max(jnp.where(acc_ref[:, :, hd:] < LIMIT, 0.0, 1.0)) < 0.5

    @pl.when(jnp.logical_not(fits))
    def _():
        again = jnp.tile(ancestors(parent_ref[...]), (groups, 1))
        for g in range(kvh):
            s = jnp.where(again, tree_scores(g), NEG)
            top = jnp.max(s, axis=1, keepdims=True)
            p = jnp.where(again, jnp.exp2(s - top), 0.0).astype(BF16)
            sh_ref[g] = jnp.broadcast_to(top, (m, 128))
            acc_ref[g] = jnp.dot(p, tree_values(g), preferred_element_type=F32)

        def step(i, carry):
            span = pl.ds(pl.multiple_of(i * sub * kvh, sub * kvh), sub * kvh)
            block = pl.ds(0, sub * kvh)
            moves = (
                pltpu.make_async_copy(k_hbm.at[span], k_raw.at[0, block], sem.at[0, 0]),
                pltpu.make_async_copy(v_hbm.at[span], v_raw.at[0, block], sem.at[1, 0]),
            )
            for move in moves:
                move.start()
            for move in moves:
                move.wait()
            k_wide[: sub * kvh] = k_raw[0, : sub * kvh].astype(F32)
            v_wide[: sub * kvh] = v_raw[0, : sub * kvh].astype(F32)
            left = length - i * sub
            col = lax.broadcasted_iota(jnp.int32, (m, sub), 1) < left
            live = lax.broadcasted_iota(jnp.int32, (sub, 128), 0) < left
            ones = jnp.where(live, 1.0, 0.0).astype(BF16)
            for g in range(kvh):
                s = dot_nt(q_ref[g], head_rows(k_wide, g, 0, sub).astype(BF16)) * scale
                s = jnp.where(col, s, NEG)
                old = sh_ref[g]
                top = jnp.maximum(old, jnp.max(s, axis=1, keepdims=True))
                shrink = jnp.exp2(old - top)
                p = [jnp.exp2(s[:, a : a + 128] - top) for a in range(0, sub, 128)]
                p = jnp.concatenate(p, axis=1).astype(BF16)
                value = jnp.where(live, head_rows(v_wide, g, 0, sub), 0.0).astype(BF16)
                value = jnp.concatenate([value, ones], axis=1)
                acc_ref[g] = acc_ref[g] * jnp.concatenate([shrink, shrink], axis=1) + jnp.dot(
                    p, value, preferred_element_type=F32
                )
                sh_ref[g] = top
            return carry

        lax.fori_loop(0, pl.cdiv(length, sub), step, 0)

    for g in range(kvh):
        rows = acc_ref[g, :, :hd] / acc_ref[g, :, hd:]
        for h in range(groups):
            lanes = slice((g * groups + h) * hd, (g * groups + h + 1) * hd)
            part = rows[h * tree : (h + 1) * tree]
            out_ref[:, lanes] = part.astype(BF16)
            of[:, lanes] = part
    for copy in small[5:]:
        copy.wait()
    for k in range(path_ref.shape[0]):
        row = of[pl.ds(nodes[0, k], 1), :]
        pf[k : k + 1, :] = jnp.where(k < plen[0], row, 0.0)
    path_ref[...] = pf[...].astype(BF16)


def attention(queries, tree_keys, tree_values, cache_keys, cache_values, lens, parent, nodes, plen):
    tree, heads, hd = queries.shape[1:]
    size, kvh = cache_keys.shape[1:3]
    groups = heads // kvh
    depth = nodes.shape[1]
    m = groups * tree
    c = min(2048, size)
    sub = min(256, c)
    flat = lambda x: x.reshape(-1, hd)
    kernel = functools.partial(
        attention_kernel,
        kvh=kvh,
        groups=groups,
        tree=tree,
        c=c,
        sub=sub,
        scale=math.log2(math.e) / math.sqrt(hd),
    )
    vmem = pl.BlockSpec(memory_space=pltpu.VMEM)
    anywhere = pl.BlockSpec(memory_space=pltpu.HBM)
    return pl.pallas_call(
        kernel,
        in_specs=[anywhere] * 9,
        out_specs=[vmem, vmem],
        scratch_shapes=[
            pltpu.SMEM((1,), jnp.int32),
            pltpu.SMEM((1, depth), jnp.int32),
            pltpu.SMEM((1,), jnp.int32),
            pltpu.VMEM((1, tree), jnp.int32),
            pltpu.VMEM((tree * kvh, hd), BF16),
            pltpu.VMEM((tree * kvh, hd), BF16),
            pltpu.VMEM((2, c * kvh, hd), BF16),
            pltpu.VMEM((2, c * kvh, hd), BF16),
            pltpu.VMEM((c * kvh, hd), F32),
            pltpu.VMEM((c * kvh, hd), F32),
            pltpu.VMEM((tree * heads, hd), BF16),
            pltpu.VMEM((tree * heads, hd), F32),
            pltpu.VMEM((kvh, m, hd), BF16),
            pltpu.VMEM((2, tree * kvh, hd), F32),
            pltpu.VMEM((2, m, c), BF16),
            pltpu.VMEM((kvh, m, 2 * hd), F32),
            pltpu.VMEM((kvh, m, 128), F32),
            pltpu.VMEM((tree, heads * hd), F32),
            pltpu.VMEM((depth, heads * hd), F32),
            pltpu.SemaphoreType.DMA((2, 2)),
            pltpu.SemaphoreType.DMA((7,)),
        ],
        out_shape=[
            jax.ShapeDtypeStruct((tree, heads * hd), BF16),
            jax.ShapeDtypeStruct((depth, heads * hd), BF16),
        ],
        name="attention",
    )(
        lens,
        nodes,
        plen,
        parent,
        flat(tree_keys),
        flat(tree_values),
        flat(queries),
        flat(cache_keys),
        flat(cache_values),
    )


def swap(x, axis, bit):
    size = lax.axis_size(axis)
    return lax.ppermute(x, axis, [(i, i ^ bit) for i in range(size)])


def bits_down(size):
    return [1 << b for b in reversed(range((size - 1).bit_length()))]


def gather_xor(x, axis):
    size = lax.axis_size(axis)
    bits = bits_down(size)
    parts, order = [x], [0]
    if size > 16:
        for bit in bits:
            x = jnp.concatenate([x, swap(x, axis, bit)], axis=0)
            order = order + [b ^ bit for b in order]
        return [x], order
    stages = [[bit] for bit in bits]
    if len(bits) > 2:
        stages = [[bits[0], bits[1], bits[0] ^ bits[1]]] + stages[2:]
    for masks in stages:
        parts = parts + [swap(part, axis, mask) for mask in masks for part in parts]
        order = order + [b ^ mask for mask in masks for b in order]
    return parts, order


def stage_kernel(*refs):
    weight, staged = refs[-2:]
    staged[...] = weight[...]


def stage(weight, after):
    vmem = pl.BlockSpec(memory_space=pltpu.VMEM)
    return pl.pallas_call(
        stage_kernel,
        in_specs=[pl.BlockSpec(memory_space=pl.ANY)] * len(after) + [vmem],
        out_specs=vmem,
        out_shape=jax.ShapeDtypeStruct(weight.shape, weight.dtype),
        compiler_params=pltpu.CompilerParams(vmem_limit_bytes=16 * 2**20),
        name="stage",
    )(*after, weight)


def project_kernel(place, *refs, order, parts, depth, mine_tokens):
    blocks = refs[:parts]
    weight, kept_ref, away_ref, rows, whole = refs[parts:]
    for at in range(parts):
        rows[at * depth : (at + 1) * depth] = blocks[at][...]
    total = jnp.dot(rows[...], weight[...], preferred_element_type=F32)
    for at, block in enumerate(order):
        row = jnp.bitwise_xor(place[0], block) * depth
        whole[pl.ds(pl.multiple_of(row, depth), depth)] = total[at * depth : (at + 1) * depth]
    kept = pl.multiple_of(place[1] * mine_tokens, mine_tokens)
    away = pl.multiple_of((1 - place[1]) * mine_tokens, mine_tokens)
    kept_ref[...] = whole[pl.ds(kept, mine_tokens)]
    away_ref[...] = whole[pl.ds(away, mine_tokens)].astype(BF16)


def project_halves(parts, order, weight, mine_tokens):
    depth, inputs = parts[0].shape
    columns = weight.shape[1]
    place = jnp.stack([lax.axis_index("dp"), lax.axis_index("tensor")]).astype(jnp.int32)
    vmem = pl.BlockSpec(memory_space=pltpu.VMEM)
    return pl.pallas_call(
        functools.partial(
            project_kernel, order=order, parts=len(parts), depth=depth, mine_tokens=mine_tokens
        ),
        in_specs=[pl.BlockSpec(memory_space=pltpu.SMEM)]
        + [vmem] * (len(parts) + 1),
        out_specs=[vmem, vmem],
        scratch_shapes=[
            pltpu.VMEM((depth * len(parts), inputs), BF16),
            pltpu.VMEM((depth * len(parts), columns), F32),
        ],
        out_shape=[
            jax.ShapeDtypeStruct((mine_tokens, columns), F32),
            jax.ShapeDtypeStruct((mine_tokens, columns), BF16),
        ],
        compiler_params=pltpu.CompilerParams(vmem_limit_bytes=16 * 2**20),
        name="project",
    )(place, *parts, weight)


def shards(
    queries,
    tree_keys,
    tree_values,
    cache_keys,
    cache_values,
    cache_len,
    tree_parent,
    path_nodes,
    path_len,
    out_weight,
    norm_gain,
):
    verify, picked = attention(
        queries, tree_keys, tree_values, cache_keys, cache_values, cache_len, tree_parent, path_nodes, path_len
    )
    dp = lax.axis_size("dp")
    tensor = lax.axis_size("tensor")
    depth = path_nodes.shape[1]
    width = dp * out_weight.shape[1]
    parts, order = gather_xor(picked, "dp")
    tokens = dp * depth // tensor
    if tensor == 2 and len(parts) == dp:
        kept, away = project_halves(parts, order, stage(out_weight, parts[:1]), tokens)
        summed = kept + swap(away, "tensor", 1).astype(F32)
    else:
        rows = jnp.concatenate(parts, axis=0)
        projected = jnp.dot(rows, out_weight, preferred_element_type=F32)
        position = [0] * dp
        for at, block in enumerate(order):
            position[block] = at
        blocks = jnp.arange(dp, dtype=jnp.int32) ^ lax.axis_index("dp")
        projected = projected.reshape(dp, depth, -1)[jnp.asarray(position, jnp.int32)[blocks]]
        projected = projected.reshape(dp * depth, -1)
        summed = lax.psum_scatter(projected.astype(BF16), "tensor", tiled=True).astype(F32)
    squares = jnp.sum(summed * summed, axis=1)
    for bit in bits_down(dp):
        squares = squares + swap(squares, "dp", bit)
    inverse = lax.rsqrt(squares / width + EPSILON)
    hidden = summed * inverse[:, None] * norm_gain[None, :]
    return (verify[None], hidden.astype(BF16))


def solution(mesh):
    return jax.shard_map(
        shards,
        mesh=mesh,
        in_specs=(
            P("dp", None, "tensor", None),
            P("dp", None, "tensor", None),
            P("dp", None, "tensor", None),
            P("dp", None, "tensor", None),
            P("dp", None, "tensor", None),
            P("dp"),
            P("dp", None),
            P("dp", None),
            P("dp"),
            P("tensor", "dp"),
            P("dp"),
        ),
        out_specs=(P("dp", None, "tensor"), P("tensor", "dp")),
        check_vma=False,
    )
```

```python
import functools
import math

import jax
import jax.numpy as jnp
from jax import lax
from jax.experimental import pallas as pl
from jax.experimental.pallas import tpu as pltpu
from jax.sharding import PartitionSpec as P

EPSILON = 1e-05
NEG = -1e30
LIMIT = 2.0**100
F32 = jnp.float32
BF16 = jnp.bfloat16


def dot_nt(a, b):
    return lax.dot_general(a, b, (((1,), (1,)), ((), ())), preferred_element_type=F32)


def ancestors(parent_row):
    t = parent_row.shape[1]
    row = lax.broadcasted_iota(jnp.int32, (t, t), 0)
    col = lax.broadcasted_iota(jnp.int32, (t, t), 1)
    reach = jnp.where((parent_row == row) | (row == col), 1.0, 0.0)
    for _ in range(max(1, (t - 1).bit_length())):
        half = reach.astype(BF16)
        reach = jnp.minimum(jnp.dot(half, half, preferred_element_type=F32), 1.0)
    return reach.T > 0.5


def attention_kernel(
    lens_hbm,
    nodes_hbm,
    plen_hbm,
    parent_hbm,
    tk_hbm,
    tv_hbm,
    q_hbm,
    k_hbm,
    v_hbm,
    out_ref,
    path_ref,
    lens,
    nodes,
    plen,
    parent_ref,
    tk_ref,
    tv_ref,
    k_raw,
    v_raw,
    k_wide,
    v_wide,
    q_raw,
    qf,
    q_ref,
    tf,
    p_ref,
    acc_ref,
    sh_ref,
    of,
    pf,
    sem,
    small_sem,
    *,
    kvh,
    groups,
    tree,
    c,
    sub,
    scale,
):
    m = groups * tree
    hd = q_ref.shape[2]
    heads = kvh * groups
    small = [
        pltpu.make_async_copy(source, target, small_sem.at[at])
        for at, (source, target) in enumerate(
            (
                (lens_hbm, lens),
                (parent_hbm, parent_ref),
                (tk_hbm, tk_ref),
                (tv_hbm, tv_ref),
                (q_hbm, q_raw),
                (nodes_hbm, nodes),
                (plen_hbm, plen),
            )
        )
    ]

    def copy_keys(n):
        span = pl.ds(pl.multiple_of(jnp.minimum(n, last) * c * kvh, c * kvh), c * kvh)
        slot = lax.rem(n, 2)
        return pltpu.make_async_copy(k_hbm.at[span], k_raw.at[slot], sem.at[0, slot])

    def copy_values(n):
        span = pl.ds(pl.multiple_of(jnp.minimum(n, last) * c * kvh, c * kvh), c * kvh)
        slot = lax.rem(n, 2)
        return pltpu.make_async_copy(v_hbm.at[span], v_raw.at[slot], sem.at[1, slot])

    for copy in small[:5]:
        copy.start()
    head = pl.ds(0, c * kvh)
    pltpu.make_async_copy(k_hbm.at[head], k_raw.at[0], sem.at[0, 0]).start()
    pltpu.make_async_copy(v_hbm.at[head], v_raw.at[0], sem.at[1, 0]).start()
    small[0].wait()
    length = lens[0]
    chunks = pl.cdiv(length, c)
    last = chunks - 1
    copy_keys(1).start()
    for copy in small[5:]:
        copy.start()

    def head_rows(ref, g, start, count):
        return ref[pl.ds(g + kvh * start, count, stride=kvh), :]

    def tree_values(g):
        value = tf[1, pl.ds(g, tree, stride=kvh), :].astype(BF16)
        return jnp.concatenate([value, jnp.ones((tree, hd), BF16)], axis=1)

    def tree_scores(g):
        keys = tf[0, pl.ds(g, tree, stride=kvh), :].astype(BF16)
        return dot_nt(q_ref[g], keys) * scale

    def widen(raw, wide):
        for i in range(c // sub):
            rows = slice(i * sub * kvh, (i + 1) * sub * kvh)
            wide[rows] = raw[rows].astype(F32)

    for copy in small[1:4]:
        copy.wait()
    tf[0] = tk_ref[...].astype(F32)
    tf[1] = tv_ref[...].astype(F32)
    allowed = jnp.tile(ancestors(parent_ref[...]), (groups, 1))
    diag_row = lax.broadcasted_iota(jnp.int32, (m, tree), 0) % tree
    diag = diag_row == lax.broadcasted_iota(jnp.int32, (m, tree), 1)
    small[4].wait()
    copy_keys(0).wait()
    widen(k_raw.at[0], k_wide)
    qf[...] = q_raw[...].astype(F32)
    for g in range(kvh):
        for h in range(groups):
            part = qf[pl.ds(g * groups + h, tree, stride=heads), :]
            q_ref[g, h * tree : (h + 1) * tree] = part.astype(BF16)
    for g in range(kvh):
        s = tree_scores(g)
        own = jnp.where(diag, s, 0.0).astype(BF16)
        shift = jnp.dot(own, jnp.ones((tree, 128), BF16), preferred_element_type=F32)
        sh_ref[g] = shift
        p = jnp.where(allowed, jnp.exp2(s - shift[:, :tree]), 0.0).astype(BF16)
        acc_ref[g] = jnp.dot(p, tree_values(g), preferred_element_type=F32)

    def absorb(n, carry):
        slot = lax.rem(n, 2)
        copy_keys(n + 1).wait()
        copy_values(n).wait()
        copy_keys(n + 2).start()
        copy_values(n + 1).start()
        live = lax.broadcasted_iota(jnp.int32, (c, 128), 0) < length - n * c
        ones = jnp.where(live, 1.0, 0.0).astype(BF16)
        for g in range(kvh):
            q = q_ref[g]
            shift = sh_ref[g]
            for i in range(c // sub):
                s = dot_nt(q, head_rows(k_wide, g, i * sub, sub).astype(BF16))
                p = [jnp.exp2(s[:, a : a + 128] * scale - shift) for a in range(0, sub, 128)]
                p_ref[g % 2, :, i * sub : (i + 1) * sub] = jnp.concatenate(p, axis=1).astype(BF16)
            if g == 0:
                widen(v_raw.at[slot], v_wide)
            if g == kvh - 1:
                widen(k_raw.at[1 - slot], k_wide)
            value = jnp.where(live, head_rows(v_wide, g, 0, c), 0.0).astype(BF16)
            value = jnp.concatenate([value, ones], axis=1)
            acc_ref[g] += jnp.dot(p_ref[g % 2], value, preferred_element_type=F32)
        return carry

    lax.fori_loop(0, chunks, absorb, 0)
    copy_keys(chunks + 1).wait()
    copy_values(chunks).wait()

    fits = jnp.max(jnp.where(acc_ref[:, :, hd:] < LIMIT, 0.0, 1.0)) < 0.5

    @pl.when(jnp.logical_not(fits))
    def _():
        again = jnp.tile(ancestors(parent_ref[...]), (groups, 1))
        for g in range(kvh):
            s = jnp.where(again, tree_scores(g), NEG)
            top = jnp.max(s, axis=1, keepdims=True)
            p = jnp.where(again, jnp.exp2(s - top), 0.0).astype(BF16)
            sh_ref[g] = jnp.broadcast_to(top, (m, 128))
            acc_ref[g] = jnp.dot(p, tree_values(g), preferred_element_type=F32)

        def step(i, carry):
            span = pl.ds(pl.multiple_of(i * sub * kvh, sub * kvh), sub * kvh)
            block = pl.ds(0, sub * kvh)
            moves = (
                pltpu.make_async_copy(k_hbm.at[span], k_raw.at[0, block], sem.at[0, 0]),
                pltpu.make_async_copy(v_hbm.at[span], v_raw.at[0, block], sem.at[1, 0]),
            )
            for move in moves:
                move.start()
            for move in moves:
                move.wait()
            k_wide[: sub * kvh] = k_raw[0, : sub * kvh].astype(F32)
            v_wide[: sub * kvh] = v_raw[0, : sub * kvh].astype(F32)
            left = length - i * sub
            col = lax.broadcasted_iota(jnp.int32, (m, sub), 1) < left
            live = lax.broadcasted_iota(jnp.int32, (sub, 128), 0) < left
            ones = jnp.where(live, 1.0, 0.0).astype(BF16)
            for g in range(kvh):
                s = dot_nt(q_ref[g], head_rows(k_wide, g, 0, sub).astype(BF16)) * scale
                s = jnp.where(col, s, NEG)
                old = sh_ref[g]
                top = jnp.maximum(old, jnp.max(s, axis=1, keepdims=True))
                shrink = jnp.exp2(old - top)
                p = [jnp.exp2(s[:, a : a + 128] - top) for a in range(0, sub, 128)]
                p = jnp.concatenate(p, axis=1).astype(BF16)
                value = jnp.where(live, head_rows(v_wide, g, 0, sub), 0.0).astype(BF16)
                value = jnp.concatenate([value, ones], axis=1)
                acc_ref[g] = acc_ref[g] * jnp.concatenate([shrink, shrink], axis=1) + jnp.dot(
                    p, value, preferred_element_type=F32
                )
                sh_ref[g] = top
            return carry

        lax.fori_loop(0, pl.cdiv(length, sub), step, 0)

    for g in range(kvh):
        rows = acc_ref[g, :, :hd] / acc_ref[g, :, hd:]
        for h in range(groups):
            lanes = slice((g * groups + h) * hd, (g * groups + h + 1) * hd)
            part = rows[h * tree : (h + 1) * tree]
            out_ref[:, lanes] = part.astype(BF16)
            of[:, lanes] = part
    for copy in small[5:]:
        copy.wait()
    for k in range(path_ref.shape[0]):
        row = of[pl.ds(nodes[0, k], 1), :]
        pf[k : k + 1, :] = jnp.where(k < plen[0], row, 0.0)
    path_ref[...] = pf[...].astype(BF16)


def attention(queries, tree_keys, tree_values, cache_keys, cache_values, lens, parent, nodes, plen):
    tree, heads, hd = queries.shape[1:]
    size, kvh = cache_keys.shape[1:3]
    groups = heads // kvh
    depth = nodes.shape[1]
    m = groups * tree
    c = min(2048, size)
    sub = min(256, c)
    flat = lambda x: x.reshape(-1, hd)
    kernel = functools.partial(
        attention_kernel,
        kvh=kvh,
        groups=groups,
        tree=tree,
        c=c,
        sub=sub,
        scale=math.log2(math.e) / math.sqrt(hd),
    )
    vmem = pl.BlockSpec(memory_space=pltpu.VMEM)
    anywhere = pl.BlockSpec(memory_space=pltpu.HBM)
    return pl.pallas_call(
        kernel,
        in_specs=[anywhere] * 9,
        out_specs=[vmem, vmem],
        scratch_shapes=[
            pltpu.SMEM((1,), jnp.int32),
            pltpu.SMEM((1, depth), jnp.int32),
            pltpu.SMEM((1,), jnp.int32),
            pltpu.VMEM((1, tree), jnp.int32),
            pltpu.VMEM((tree * kvh, hd), BF16),
            pltpu.VMEM((tree * kvh, hd), BF16),
            pltpu.VMEM((2, c * kvh, hd), BF16),
            pltpu.VMEM((2, c * kvh, hd), BF16),
            pltpu.VMEM((c * kvh, hd), F32),
            pltpu.VMEM((c * kvh, hd), F32),
            pltpu.VMEM((tree * heads, hd), BF16),
            pltpu.VMEM((tree * heads, hd), F32),
            pltpu.VMEM((kvh, m, hd), BF16),
            pltpu.VMEM((2, tree * kvh, hd), F32),
            pltpu.VMEM((2, m, c), BF16),
            pltpu.VMEM((kvh, m, 2 * hd), F32),
            pltpu.VMEM((kvh, m, 128), F32),
            pltpu.VMEM((tree, heads * hd), F32),
            pltpu.VMEM((depth, heads * hd), F32),
            pltpu.SemaphoreType.DMA((2, 2)),
            pltpu.SemaphoreType.DMA((7,)),
        ],
        out_shape=[
            jax.ShapeDtypeStruct((tree, heads * hd), BF16),
            jax.ShapeDtypeStruct((depth, heads * hd), BF16),
        ],
        name="attention",
    )(
        lens,
        nodes,
        plen,
        parent,
        flat(tree_keys),
        flat(tree_values),
        flat(queries),
        flat(cache_keys),
        flat(cache_values),
    )


def swap(x, axis, bit):
    size = lax.axis_size(axis)
    return lax.ppermute(x, axis, [(i, i ^ bit) for i in range(size)])


def bits_down(size):
    return [1 << b for b in reversed(range((size - 1).bit_length()))]


def gather_xor(x, axis):
    size = lax.axis_size(axis)
    bits = bits_down(size)
    parts, order = [x], [0]
    if size > 16:
        for bit in bits:
            x = jnp.concatenate([x, swap(x, axis, bit)], axis=0)
            order = order + [b ^ bit for b in order]
        return [x], order
    stages = [[bit] for bit in bits]
    if len(bits) > 2:
        stages = [[bits[0], bits[1], bits[0] ^ bits[1]]] + stages[2:]
    for masks in stages:
        parts = parts + [swap(part, axis, mask) for mask in masks for part in parts]
        order = order + [b ^ mask for mask in masks for b in order]
    return parts, order


def stage_kernel(*refs):
    weight, staged = refs[-2:]
    staged[...] = weight[...]


def stage(weight, after):
    vmem = pl.BlockSpec(memory_space=pltpu.VMEM)
    return pl.pallas_call(
        stage_kernel,
        in_specs=[pl.BlockSpec(memory_space=pl.ANY)] * len(after) + [vmem],
        out_specs=vmem,
        out_shape=jax.ShapeDtypeStruct(weight.shape, weight.dtype),
        compiler_params=pltpu.CompilerParams(vmem_limit_bytes=16 * 2**20),
        name="stage",
    )(*after, weight)


def project_kernel(place, *refs, order, parts, depth, mine_tokens):
    blocks = refs[:parts]
    weight, kept_ref, away_ref, rows, whole = refs[parts:]
    for at in range(parts):
        rows[at * depth : (at + 1) * depth] = blocks[at][...]
    total = jnp.dot(rows[...], weight[...], preferred_element_type=F32)
    for at, block in enumerate(order):
        row = jnp.bitwise_xor(place[0], block) * depth
        whole[pl.ds(pl.multiple_of(row, depth), depth)] = total[at * depth : (at + 1) * depth]
    kept = pl.multiple_of(place[1] * mine_tokens, mine_tokens)
    away = pl.multiple_of((1 - place[1]) * mine_tokens, mine_tokens)
    kept_ref[...] = whole[pl.ds(kept, mine_tokens)]
    away_ref[...] = whole[pl.ds(away, mine_tokens)].astype(BF16)


def project_halves(parts, order, weight, mine_tokens):
    depth, inputs = parts[0].shape
    columns = weight.shape[1]
    place = jnp.stack([lax.axis_index("dp"), lax.axis_index("tensor")]).astype(jnp.int32)
    vmem = pl.BlockSpec(memory_space=pltpu.VMEM)
    return pl.pallas_call(
        functools.partial(
            project_kernel, order=order, parts=len(parts), depth=depth, mine_tokens=mine_tokens
        ),
        in_specs=[pl.BlockSpec(memory_space=pltpu.SMEM)]
        + [vmem] * (len(parts) + 1),
        out_specs=[vmem, vmem],
        scratch_shapes=[
            pltpu.VMEM((depth * len(parts), inputs), BF16),
            pltpu.VMEM((depth * len(parts), columns), F32),
        ],
        out_shape=[
            jax.ShapeDtypeStruct((mine_tokens, columns), F32),
            jax.ShapeDtypeStruct((mine_tokens, columns), BF16),
        ],
        compiler_params=pltpu.CompilerParams(vmem_limit_bytes=16 * 2**20),
        name="project",
    )(place, *parts, weight)


def shards(
    queries,
    tree_keys,
    tree_values,
    cache_keys,
    cache_values,
    cache_len,
    tree_parent,
    path_nodes,
    path_len,
    out_weight,
    norm_gain,
):
    verify, picked = attention(
        queries, tree_keys, tree_values, cache_keys, cache_values, cache_len, tree_parent, path_nodes, path_len
    )
    dp = lax.axis_size("dp")
    tensor = lax.axis_size("tensor")
    depth = path_nodes.shape[1]
    width = dp * out_weight.shape[1]
    parts, order = gather_xor(picked, "dp")
    tokens = dp * depth // tensor
    if tensor == 2 and len(parts) == dp:
        kept, away = project_halves(parts, order, stage(out_weight, parts[3:4]), tokens)
        summed = kept + swap(away, "tensor", 1).astype(F32)
    else:
        rows = jnp.concatenate(parts, axis=0)
        projected = jnp.dot(rows, out_weight, preferred_element_type=F32)
        position = [0] * dp
        for at, block in enumerate(order):
            position[block] = at
        blocks = jnp.arange(dp, dtype=jnp.int32) ^ lax.axis_index("dp")
        projected = projected.reshape(dp, depth, -1)[jnp.asarray(position, jnp.int32)[blocks]]
        projected = projected.reshape(dp * depth, -1)
        summed = lax.psum_scatter(projected.astype(BF16), "tensor", tiled=True).astype(F32)
    squares = jnp.sum(summed * summed, axis=1)
    for bit in bits_down(dp):
        squares = squares + swap(squares, "dp", bit)
    inverse = lax.rsqrt(squares / width + EPSILON)
    hidden = summed * inverse[:, None] * norm_gain[None, :]
    return (verify[None], hidden.astype(BF16))


def solution(mesh):
    return jax.shard_map(
        shards,
        mesh=mesh,
        in_specs=(
            P("dp", None, "tensor", None),
            P("dp", None, "tensor", None),
            P("dp", None, "tensor", None),
            P("dp", None, "tensor", None),
            P("dp", None, "tensor", None),
            P("dp"),
            P("dp", None),
            P("dp", None),
            P("dp"),
            P("tensor", "dp"),
            P("dp"),
        ),
        out_specs=(P("dp", None, "tensor"), P("tensor", "dp")),
        check_vma=False,
    )
```
